32 devices in a mesh: groups: 2 (over x), row: 16 (over z, y, core).
Axes of the slice: x: 2, y: 2, z: 4, core: 2. Of those that a mesh axis runs over, the one named last changes fastest.
Arguments:
- forces: bfloat16 [2048, 768], P(('groups', 'row')), parts along dimension 0, may hold values from -6 to 6
- tiles: bfloat16 [32768, 96, 96], P(('groups', 'row')), parts along dimension 0, may hold values from -0.109375 to 0.109375
- tile_local: int32 [32768], P(('groups', 'row')), parts along dimension 0, may hold values from 0 to 63
- tile_slot: int32 [32768], P(('groups', 'row')), parts along dimension 0, may hold values from 0 to 255
- tile_flag: int32 [32768], P(('groups', 'row')), parts along dimension 0, may hold values 0 or 1
- want_list: int32 [32, 16, 16], P(('groups', 'row')), parts along dimension 0, may hold values from 0 to 63
Outputs:
- krylov_one: bfloat16 [2048, 768], P(('groups', 'row')), parts along dimension 0
- krylov_two: bfloat16 [2048, 768], P(('groups', 'row')), parts along dimension 0
The draws below stay inside these ranges and needn't reach their ends.
There are 2 independent parts, one for each index of `groups`. The reference program is written for one: setup_inputs(seed, part) draws one part's arguments, and reference() takes and returns one part's arrays. A program takes and returns all parts, laid end to end along the dimension named above; each array names one. Nothing has to cross between parts.
All inputs are finite; a program needn't handle non-finite values. No bound on the sum of `tile_flag` on one device may be relied on, other than what follows from the above.
Results may differ from the reference program's by a relative error of at most 0.0041.
Values may be sent and summed in bfloat16 or wider, within the bound.
No kernel may reach another device: no remote copies, remote signals or barrier semaphores. Data moves between devices by JAX's collectives and lax.ppermute only.
A program may use at most 128 MiB of HBM per device.

```python
import jax
import jax.numpy as jnp
from jax import lax

UNK = 96
NRHS = 8
WIDTH = 768
FD = 64
TILE_DEV = 1024
CAP = 16
BLOCKS = 16
FIBRES = 1024
TILES = 16384
SLOTS = 256
N_ROW = 16


def set_ends(result, rng, low, high):
    index_at = [jax.random.randint(jax.random.fold_in(rng, axis), (), 0, length) for axis, length in enumerate(result.shape)]
    longest = result.shape.index(max(result.shape))
    next_to = index_at[:longest] + [(index_at[longest] + 1) % result.shape[longest]] + index_at[longest + 1:]
    return result.at[tuple(index_at)].set(low).at[tuple(next_to)].set(high)


def shard_levels(stream_key, shape, cuts, least, top_value):
    def one(dim, blocks):
        draws = jax.random.uniform(jax.random.fold_in(jax.random.fold_in(stream_key, 6), dim), (blocks,), jnp.float32, least / len(cuts), top_value / len(cuts))
        return jnp.repeat(jnp.exp(draws), shape[dim] // blocks).reshape((-1,) + (1,) * (len(shape) - dim - 1))

    level = one(*cuts[0])
    for cut in cuts[1:]:
        level = level * one(*cut)
    return level


def noise(rng, shape, spread, reach, split=(), kind=jnp.bfloat16):
    array = spread * jax.random.normal(rng, shape, jnp.float32)
    if split:
        array = array * shard_levels(rng, shape, split, -0.22, 0.18)
    return jnp.clip(array, -reach, reach).astype(kind)


def setup_inputs(seed: int = 0, part: int = 0) -> dict:
    splits = jax.random.split(jax.random.key(seed), 7)
    own_keys = jax.random.split(jax.random.fold_in(splits[6], part), 7)
    forces = noise(own_keys[0], (FIBRES, WIDTH), 1.0, 6.0, ((0, 16),))
    tiles = noise(own_keys[1], (TILES, UNK, UNK), (UNK * 2 * TILE_DEV // FD) ** -0.5, 0.109375, ((0, 16),))
    tile_local = set_ends(jax.random.randint(own_keys[2], (TILES,), 0, FD), jax.random.fold_in(own_keys[2], 1), 0, FD - 1).astype(jnp.int32)
    tile_slot = set_ends(jax.random.randint(own_keys[3], (TILES,), 0, SLOTS), jax.random.fold_in(own_keys[3], 1), 0, SLOTS - 1).astype(jnp.int32)
    tile_flag = set_ends((jax.random.randint(own_keys[4], (TILES,), 0, 4) < 3).astype(jnp.int32), jax.random.fold_in(own_keys[4], 1), 0, 1)
    want_list = set_ends(jax.random.randint(own_keys[5], (BLOCKS, BLOCKS, CAP), 0, FD), jax.random.fold_in(own_keys[5], 1), 0, FD - 1).astype(jnp.int32)
    return {"forces": forces, "tiles": tiles, "tile_local": tile_local, "tile_slot": tile_slot, "tile_flag": tile_flag, "want_list": want_list}


def apply_mobility(field, tiles, tile_local, tile_slot, tile_flag, want_list):
    tile_blocks = tiles.reshape(N_ROW, TILE_DEV, UNK, UNK)
    local_blocks = tile_local.reshape(N_ROW, TILE_DEV)
    slot_blocks = tile_slot.reshape(N_ROW, TILE_DEV)
    flag_blocks = tile_flag.reshape(N_ROW, TILE_DEV)
    block_ids = jnp.arange(N_ROW, dtype=jnp.int32)

    def step(total, inputs):
        blocks, local, slot, flag, wanted, block_id = inputs
        peer = (slot // CAP).astype(jnp.int32)
        column = (slot % CAP).astype(jnp.int32)
        far_rows = (peer * FD + wanted[peer, column]).astype(jnp.int32)
        near_rows = (block_id * FD + local).astype(jnp.int32)
        far_vals = field[far_rows].astype(jnp.float32).reshape(TILE_DEV, NRHS, UNK)
        near_vals = field[near_rows].astype(jnp.float32).reshape(TILE_DEV, NRHS, UNK)
        tiles_wide = blocks.astype(jnp.float32)
        direct = jnp.einsum("kij,krj->kri", tiles_wide, far_vals, precision=lax.Precision.HIGHEST)
        mirror = jnp.einsum("kij,kri->krj", tiles_wide, near_vals, precision=lax.Precision.HIGHEST)
        mirror = mirror * flag.astype(jnp.float32)[:, None, None]
        total = total.at[near_rows].add(direct.reshape(TILE_DEV, WIDTH))
        total = total.at[far_rows].add(mirror.reshape(TILE_DEV, WIDTH))
        return total, None

    start = jnp.zeros((FIBRES, WIDTH), jnp.float32)
    total, unused = lax.scan(step, start, (tile_blocks, local_blocks, slot_blocks, flag_blocks, want_list, block_ids))
    return total


def reference(forces, tiles, tile_local, tile_slot, tile_flag, want_list):
    krylov_one = apply_mobility(forces, tiles, tile_local, tile_slot, tile_flag, want_list).astype(jnp.bfloat16)
    krylov_two = apply_mobility(krylov_one, tiles, tile_local, tile_slot, tile_flag, want_list).astype(jnp.bfloat16)
    return (krylov_one, krylov_two)
```

```python
import functools

import jax
import jax.numpy as jnp
from jax import lax
from jax.experimental import pallas as pl
from jax.experimental.pallas import tpu as pltpu
from jax.sharding import PartitionSpec as P

NRHS = 8
LANES = 128
PAIRS_PER_STEP = 32
QUADS_PER_LOOP = 4
VMEM_LIMIT = 40 * 1024 * 1024


def mirror_kernel(first, unknowns, slots, own_at, slot_at, tile_ref, field_ref, *rest):
    if first:
        slot_ref, wide_ref, near_ref, sum_ref = rest
    else:
        slot_ref, near_ref, sum_ref = rest
    step = pl.program_id(0)
    fibres = field_ref.shape[0]
    depth = 2 * unknowns

    @pl.when(step == 0)
    def _():
        sum_ref[...] = jnp.zeros_like(sum_ref)
        field = field_ref[...].astype(jnp.float32)
        blank = jnp.zeros((fibres, unknowns), jnp.float32)
        for r in range(NRHS):
            part = field[:, r * unknowns : (r + 1) * unknowns]
            near_ref[:fibres, r, :] = jnp.concatenate([part, blank], axis=1)
            near_ref[fibres:, r, :] = jnp.concatenate([blank, part], axis=1)

    def quads(loop, carry):
        found = []
        for u in range(QUADS_PER_LOOP):
            pair = (loop * QUADS_PER_LOOP + u) * 2
            tile = (step * PAIRS_PER_STEP + pair) * 2
            halves = []
            for h in range(2):
                half = tile_ref[pair + h]
                if first:
                    half = jnp.concatenate(
                        [half, jnp.zeros((depth, LANES - unknowns), half.dtype)], axis=1
                    )
                    wide_ref[pair + h] = half
                halves.append(half)
            left = jnp.concatenate(
                [near_ref[own_at[tile + t]] for t in range(4)], axis=0
            ).astype(jnp.bfloat16)
            right = jnp.concatenate(halves, axis=1)
            found.append(jnp.dot(left, right, preferred_element_type=jnp.float32))
        for u in range(QUADS_PER_LOOP):
            tile = (step * PAIRS_PER_STEP + (loop * QUADS_PER_LOOP + u) * 2) * 2
            for t in range(4):
                lane = (t // 2) * LANES
                slot = slot_at[tile + t]
                sum_ref[slot] += found[u][t * NRHS : (t + 1) * NRHS, lane : lane + LANES]
        return carry

    lax.fori_loop(0, PAIRS_PER_STEP // (2 * QUADS_PER_LOOP), quads, 0)

    @pl.when(step == pl.num_programs(0) - 1)
    def _():
        rows = [sum_ref[:slots, r, :][:, :unknowns] for r in range(NRHS)]
        slot_ref[...] = jnp.concatenate(rows, axis=1).astype(slot_ref.dtype)


def mirror(first, tiles, field, own_at, slot_at, slots):
    pairs, depth, width = tiles.shape
    unknowns = depth // 2
    fibres = field.shape[0]
    steps = pairs // PAIRS_PER_STEP
    tile_spec = pl.BlockSpec((PAIRS_PER_STEP, depth, width), lambda i, *_: (i, 0, 0))
    wide_spec = pl.BlockSpec((PAIRS_PER_STEP, depth, LANES), lambda i, *_: (i, 0, 0))
    out_shape = [jax.ShapeDtypeStruct((slots, field.shape[1]), jnp.bfloat16)]
    out_specs = [pl.BlockSpec((slots, field.shape[1]), lambda i, *_: (0, 0))]
    if first:
        out_shape.append(jax.ShapeDtypeStruct((pairs, depth, LANES), tiles.dtype))
        out_specs.append(wide_spec)
    return pl.pallas_call(
        functools.partial(mirror_kernel, first, unknowns, slots),
        out_shape=out_shape,
        grid_spec=pltpu.PrefetchScalarGridSpec(
            num_scalar_prefetch=2,
            grid=(steps,),
            in_specs=[tile_spec, pl.BlockSpec(field.shape, lambda i, *_: (0, 0))],
            out_specs=out_specs,
            scratch_shapes=[
                pltpu.VMEM((2 * fibres, NRHS, depth), jnp.float32),
                pltpu.VMEM((slots + 1, NRHS, LANES), jnp.float32),
            ],
        ),
        compiler_params=pltpu.CompilerParams(vmem_limit_bytes=VMEM_LIMIT),
        cost_estimate=pl.CostEstimate(
            flops=4 * pairs * depth * NRHS * unknowns,
            bytes_accessed=2 * pairs * depth * LANES * (2 if first else 1),
            transcendentals=0,
        ),
        name="mirror_first" if first else "mirror",
    )(own_at, slot_at, tiles, field)


def direct_kernel(unknowns, own_at, slot_at, tile_ref, field_ref, own_ref, far_ref, even_ref, odd_ref):
    step = pl.program_id(0)
    slots = field_ref.shape[0]

    @pl.when(step == 0)
    def _():
        even_ref[...] = jnp.zeros_like(even_ref)
        odd_ref[...] = jnp.zeros_like(odd_ref)
        field = field_ref[...].astype(jnp.float32)
        blank = jnp.zeros((slots, LANES - unknowns), jnp.float32)
        for r in range(NRHS):
            part = field[:, r * unknowns : (r + 1) * unknowns]
            far_ref[:, r, :] = jnp.concatenate([part, blank], axis=1)

    none = jnp.zeros((NRHS, LANES), jnp.float32)

    def quads(loop, carry):
        found = []
        for u in range(QUADS_PER_LOOP):
            pair = (loop * QUADS_PER_LOOP + u) * 2
            tile = (step * PAIRS_PER_STEP + pair) * 2
            far = [far_ref[slot_at[tile + t]] for t in range(4)]
            left = jnp.concatenate(
                [
                    jnp.concatenate(far[:2] + [none, none], axis=0),
                    jnp.concatenate([none, none] + far[2:], axis=0),
                ],
                axis=1,
            ).astype(jnp.bfloat16)
            right = jnp.concatenate([tile_ref[pair], tile_ref[pair + 1]], axis=1)
            found.append(
                lax.dot_general(
                    left, right, (((1,), (1,)), ((), ())), preferred_element_type=jnp.float32
                )
            )
        for u in range(QUADS_PER_LOOP):
            tile = (step * PAIRS_PER_STEP + (loop * QUADS_PER_LOOP + u) * 2) * 2
            for t in range(4):
                rows = found[u][t * NRHS : (t + 1) * NRHS]
                own = own_at[tile + t]
                if t % 2 == 0:
                    even_ref[own] += rows[:, :LANES]
                else:
                    odd_ref[own] += rows
        return carry

    lax.fori_loop(0, PAIRS_PER_STEP // (2 * QUADS_PER_LOOP), quads, 0)

    @pl.when(step == pl.num_programs(0) - 1)
    def _():
        rows = [
            even_ref[:, r, :][:, :unknowns] + odd_ref[:, r, :][:, unknowns:]
            for r in range(NRHS)
        ]
        own_ref[...] = jnp.concatenate(rows, axis=1)


def direct(tiles, field, own_at, slot_at, fibres):
    pairs, depth, width = tiles.shape
    unknowns = depth // 2
    slots = field.shape[0]
    return pl.pallas_call(
        functools.partial(direct_kernel, unknowns),
        out_shape=jax.ShapeDtypeStruct((fibres, field.shape[1]), jnp.float32),
        grid_spec=pltpu.PrefetchScalarGridSpec(
            num_scalar_prefetch=2,
            grid=(pairs // PAIRS_PER_STEP,),
            in_specs=[
                pl.BlockSpec((PAIRS_PER_STEP, depth, width), lambda i, *_: (i, 0, 0)),
                pl.BlockSpec(field.shape, lambda i, *_: (0, 0)),
            ],
            out_specs=pl.BlockSpec((fibres, field.shape[1]), lambda i, *_: (0, 0)),
            scratch_shapes=[
                pltpu.VMEM((slots, NRHS, LANES), jnp.float32),
                pltpu.VMEM((fibres, NRHS, LANES), jnp.float32),
                pltpu.VMEM((fibres, NRHS, depth), jnp.float32),
            ],
        ),
        compiler_params=pltpu.CompilerParams(vmem_limit_bytes=VMEM_LIMIT),
        cost_estimate=pl.CostEstimate(
            flops=4 * pairs * depth * NRHS * unknowns,
            bytes_accessed=2 * pairs * depth * LANES,
            transcendentals=0,
        ),
        name="direct",
    )(own_at, slot_at, tiles, field)


def per_device(forces, tiles, tile_local, tile_slot, tile_flag, want_list):
    fibres, row_width = forces.shape
    blocks, unknowns, _ = tiles.shape
    _, peers, capacity = want_list.shape
    slots = peers * capacity

    def exchange(rows):
        return lax.all_to_all(rows, "row", 0, 0)

    asked = exchange(want_list[0]).reshape(slots)
    asked_pick = (asked[:, None] == jnp.arange(fibres, dtype=jnp.int32)[None, :]).astype(
        jnp.bfloat16
    )
    mirror_own = tile_local + fibres * (jnp.arange(blocks, dtype=jnp.int32) % 2)
    mirror_slot = jnp.where(tile_flag == 1, tile_slot, slots)

    def fetch(current):
        rows = jnp.dot(asked_pick, current, preferred_element_type=jnp.float32)
        rows = rows.astype(jnp.bfloat16).reshape(peers, capacity, row_width)
        return exchange(rows).reshape(slots, row_width)

    def give_back(slot_part):
        back = exchange(slot_part.reshape(peers, capacity, row_width)).reshape(slots, row_width)
        return lax.dot_general(
            asked_pick, back, (((0,), (0,)), ((), ())), preferred_element_type=jnp.float32
        )

    far = fetch(forces)
    slot_part, wide = mirror(
        True, tiles.reshape(blocks // 2, 2 * unknowns, unknowns), forces, mirror_own, mirror_slot, slots
    )
    own_part = direct(wide, far, tile_local, tile_slot, fibres)
    krylov_one = (own_part + give_back(slot_part)).astype(jnp.bfloat16)

    far = fetch(krylov_one)
    (slot_part,) = mirror(False, wide, krylov_one, mirror_own, mirror_slot, slots)
    own_part = direct(wide, far, tile_local, tile_slot, fibres)
    krylov_two = (own_part + give_back(slot_part)).astype(jnp.bfloat16)
    return (krylov_one, krylov_two)


def solution(mesh):
    spec = ("groups", "row")
    in_specs = (
        P(spec, None),
        P(spec, None, None),
        P(spec),
        P(spec),
        P(spec),
        P(spec, None, None),
    )
    out_specs = (P(spec, None), P(spec, None))
    return jax.shard_map(
        per_device, mesh=mesh, in_specs=in_specs, out_specs=out_specs, check_vma=False
    )
```

```python
import jax
import jax.numpy as jnp
from jax import lax
from jax.experimental import pallas as pl
from jax.experimental.pallas import tpu as pltpu
from jax.sharding import PartitionSpec as P

NRHS = 8
LANES = 128
QUADS_PER_LOOP = 16
NOTE_ROWS = 16
PAIRS_PER_CHUNK = 64
CHUNKS_HELD = 3
STRIDE_PAD = 1
RELAY_LOOPS = 4
TILE_BLOCK = 128
RELAY_VMEM = 26 * 1024 * 1024
PRODUCT_VMEM = 20 * 1024 * 1024


def relay_kernel(native_ref, wide_ref, line_ref):
    step = pl.program_id(0)
    last = pl.num_programs(0) - 1
    unknowns = native_ref.shape[0]
    block = native_ref.shape[2]
    stride = block + STRIDE_PAD
    lines = unknowns * stride
    put_at = (step % 2) * lines
    take_at = ((step + 1) % 2) * lines
    blank = jnp.zeros((LANES - unknowns, block), native_ref.dtype)
    rows = unknowns // RELAY_LOOPS
    pairs = block // (2 * RELAY_LOOPS)

    def turn(loop):
        for u in range(rows):
            i = loop * rows + u
            wide = jnp.concatenate([native_ref[i], blank], axis=0)
            line_ref[pl.ds(put_at + i * stride, block), :] = wide.T.astype(jnp.float32)

    def collect(loop):
        for u in range(pairs):
            pair = loop * pairs + u
            for h in range(2):
                lines_of = pl.ds(take_at + 2 * pair + h, unknowns, stride=stride)
                wide_ref[pair, h * unknowns : (h + 1) * unknowns, :] = line_ref[
                    lines_of, :
                ].astype(wide_ref.dtype)

    def run(*parts):
        def body(loop, carry):
            for part in parts:
                part(loop)
            return carry

        lax.fori_loop(0, RELAY_LOOPS, body, 0)

    @pl.when(step == 0)
    def _():
        run(turn)

    @pl.when(jnp.logical_and(step > 0, step < last))
    def _():
        run(collect, turn)

    @pl.when(step == last)
    def _():
        run(collect)


def relay(native):
    unknowns, _, blocks = native.shape
    steps = blocks // TILE_BLOCK
    return pl.pallas_call(
        relay_kernel,
        out_shape=pltpu.HBM((blocks // 2, 2 * unknowns, LANES), native.dtype),
        grid=(steps + 1,),
        in_specs=[
            pl.BlockSpec(
                (unknowns, unknowns, TILE_BLOCK), lambda i: (0, 0, jnp.minimum(i, steps - 1))
            )
        ],
        out_specs=pl.BlockSpec(
            (TILE_BLOCK // 2, 2 * unknowns, LANES), lambda i: (jnp.maximum(i - 1, 0), 0, 0)
        ),
        scratch_shapes=[
            pltpu.VMEM((2 * unknowns * (TILE_BLOCK + STRIDE_PAD), LANES), jnp.float32)
        ],
        compiler_params=pltpu.CompilerParams(vmem_limit_bytes=RELAY_VMEM),
        cost_estimate=pl.CostEstimate(
            flops=0, bytes_accessed=8 * blocks * unknowns * LANES, transcendentals=0
        ),
        name="relay",
    )(pltpu.with_memory_space_constraint(native, pltpu.HBM))


def chunk_copy(tile_ref, held_ref, ready, chunk):
    slot = chunk % CHUNKS_HELD
    return pltpu.make_async_copy(
        tile_ref.at[pl.ds(chunk * PAIRS_PER_CHUNK, PAIRS_PER_CHUNK)],
        held_ref.at[slot],
        ready.at[slot],
    )


def open_stream(tile_ref, held_ref, ready):
    for chunk in range(CHUNKS_HELD - 1):
        chunk_copy(tile_ref, held_ref, ready, chunk).start()


def run_stream(tile_ref, held_ref, ready, quads):
    chunks = tile_ref.shape[0] // PAIRS_PER_CHUNK

    def body(chunk, carry):
        chunk_copy(tile_ref, held_ref, ready, chunk).wait()

        @pl.when(chunk + CHUNKS_HELD - 1 < chunks)
        def _():
            chunk_copy(tile_ref, held_ref, ready, chunk + CHUNKS_HELD - 1).start()

        held = held_ref.at[chunk % CHUNKS_HELD]

        def inner(loop, carry):
            quads(held, loop * 2 * QUADS_PER_LOOP, chunk * PAIRS_PER_CHUNK)
            return carry

        return lax.fori_loop(0, PAIRS_PER_CHUNK // (2 * QUADS_PER_LOOP), inner, carry)

    lax.fori_loop(0, chunks, body, 0)


def mirror_kernel(
    own_at, slot_at, tile_ref, field_ref, slot_ref, held_ref, ready, near_ref, sum_ref
):
    open_stream(tile_ref, held_ref, ready)
    fibres, width = field_ref.shape
    slots = slot_ref.shape[0]
    unknowns = width // NRHS
    sum_ref[...] = jnp.zeros_like(sum_ref)
    field = field_ref[...].astype(jnp.float32)
    blank = jnp.zeros((fibres, unknowns), jnp.float32)
    for r in range(NRHS):
        part = field[:, r * unknowns : (r + 1) * unknowns]
        near_ref[:fibres, r, :] = jnp.concatenate([part, blank], axis=1)
        near_ref[fibres:, r, :] = jnp.concatenate([blank, part], axis=1)

    def quads(held, pair_at, chunk_at):
        first = 2 * (chunk_at + pair_at)
        found = []
        for u in range(QUADS_PER_LOOP):
            pair = pair_at + 2 * u
            left = jnp.concatenate(
                [near_ref[own_at[first + 4 * u + t]] for t in range(4)], axis=0
            ).astype(jnp.bfloat16)
            right = jnp.concatenate([held[pair], held[pair + 1]], axis=1)
            found.append(jnp.dot(left, right, preferred_element_type=jnp.float32))
        for u in range(QUADS_PER_LOOP):
            for t in range(4):
                lane = (t // 2) * LANES
                slot = slot_at[first + 4 * u + t]
                sum_ref[slot] += found[u][t * NRHS : (t + 1) * NRHS, lane : lane + LANES]

    run_stream(tile_ref, held_ref, ready, quads)
    rows = [sum_ref[:slots, r, :][:, :unknowns] for r in range(NRHS)]
    slot_ref[...] = jnp.concatenate(rows, axis=1).astype(slot_ref.dtype)


def product_call(kernel, name, tiles, field, own_at, slot_at, out_shape, scratch_shapes):
    pairs, depth, _ = tiles.shape
    whole = pl.BlockSpec(memory_space=pltpu.VMEM)
    stay = pl.BlockSpec(memory_space=pltpu.HBM)
    stream_shapes = [
        pltpu.VMEM((CHUNKS_HELD, PAIRS_PER_CHUNK, depth, LANES), tiles.dtype),
        pltpu.SemaphoreType.DMA((CHUNKS_HELD,)),
    ]
    index = pl.BlockSpec(memory_space=pltpu.SMEM)
    return pl.pallas_call(
        kernel,
        out_shape=out_shape,
        in_specs=[index, index, stay, whole],
        out_specs=whole,
        scratch_shapes=stream_shapes + scratch_shapes,
        compiler_params=pltpu.CompilerParams(vmem_limit_bytes=PRODUCT_VMEM),
        cost_estimate=pl.CostEstimate(
            flops=4 * pairs * depth * NRHS * LANES,
            bytes_accessed=2 * pairs * depth * LANES,
            transcendentals=0,
        ),
        name=name,
    )(own_at, slot_at, pltpu.with_memory_space_constraint(tiles, pltpu.HBM), field)


def mirror(tiles, field, own_at, slot_at, slots):
    fibres, width = field.shape
    return product_call(
        mirror_kernel,
        "mirror",
        tiles,
        field,
        own_at,
        slot_at,
        jax.ShapeDtypeStruct((slots, width), jnp.bfloat16),
        [
            pltpu.VMEM((2 * fibres, NRHS, tiles.shape[1]), jnp.float32),
            pltpu.VMEM((slots + 1, NRHS, LANES), jnp.float32),
        ],
    )


def direct_kernel(
    own_at, slot_at, tile_ref, field_ref, own_ref, held_ref, ready, far_ref, even_ref, odd_ref
):
    open_stream(tile_ref, held_ref, ready)
    slots, width = field_ref.shape
    unknowns = width // NRHS
    even_ref[...] = jnp.zeros_like(even_ref)
    odd_ref[...] = jnp.zeros_like(odd_ref)
    field = field_ref[...].astype(jnp.float32)
    blank = jnp.zeros((slots, LANES - unknowns), jnp.float32)
    for r in range(NRHS):
        part = field[:, r * unknowns : (r + 1) * unknowns]
        far_ref[:, r, :] = jnp.concatenate([part, blank], axis=1)

    none = jnp.zeros((NRHS, LANES), jnp.float32)

    def quads(held, pair_at, chunk_at):
        first = 2 * (chunk_at + pair_at)
        found = []
        for u in range(QUADS_PER_LOOP):
            pair = pair_at + 2 * u
            far = [far_ref[slot_at[first + 4 * u + t]] for t in range(4)]
            left = jnp.concatenate(
                [
                    jnp.concatenate(far[:2] + [none, none], axis=0),
                    jnp.concatenate([none, none] + far[2:], axis=0),
                ],
                axis=1,
            ).astype(jnp.bfloat16)
            right = jnp.concatenate([held[pair], held[pair + 1]], axis=1)
            found.append(
                lax.dot_general(
                    left, right, (((1,), (1,)), ((), ())), preferred_element_type=jnp.float32
                )
            )
        for u in range(QUADS_PER_LOOP):
            for t in range(4):
                rows = found[u][t * NRHS : (t + 1) * NRHS]
                own = own_at[first + 4 * u + t]
                if t % 2 == 0:
                    even_ref[own] += rows[:, :LANES]
                else:
                    odd_ref[own] += rows

    run_stream(tile_ref, held_ref, ready, quads)
    rows = [
        even_ref[:, r, :][:, :unknowns] + odd_ref[:, r, :][:, unknowns:] for r in range(NRHS)
    ]
    own_ref[...] = jnp.concatenate(rows, axis=1)


def direct(tiles, field, own_at, slot_at, fibres):
    slots, width = field.shape
    return product_call(
        direct_kernel,
        "direct",
        tiles,
        field,
        own_at,
        slot_at,
        jax.ShapeDtypeStruct((fibres, width), jnp.float32),
        [
            pltpu.VMEM((slots, NRHS, LANES), jnp.float32),
            pltpu.VMEM((fibres, NRHS, LANES), jnp.float32),
            pltpu.VMEM((fibres, NRHS, tiles.shape[1]), jnp.float32),
        ],
    )


def per_device(forces, tiles, tile_local, tile_slot, tile_flag, want_list):
    fibres, row_width = forces.shape
    blocks = tiles.shape[0]
    _, peers, capacity = want_list.shape
    slots = peers * capacity

    def exchange(rows):
        return lax.all_to_all(rows, "row", 0, 0)

    me = lax.axis_index("row")
    notes = want_list[0].astype(jnp.bfloat16).reshape(1, slots)
    notes = jnp.pad(notes, ((0, NOTE_ROWS - 1), (0, row_width - slots)))
    everyone = lax.all_gather(jnp.concatenate([forces, notes], axis=0), "row")
    wanted = everyone[:, fibres, :slots].reshape(peers, peers, capacity)
    asked = lax.dynamic_index_in_dim(wanted, me, 1, False).astype(jnp.int32).reshape(slots)
    asked_pick = (asked[:, None] == jnp.arange(fibres, dtype=jnp.int32)[None, :]).astype(
        jnp.bfloat16
    )
    mirror_own = tile_local + fibres * (jnp.arange(blocks, dtype=jnp.int32) % 2)
    mirror_slot = jnp.where(tile_flag == 1, tile_slot, slots)

    def fetch(current):
        rows = jnp.dot(asked_pick, current, preferred_element_type=jnp.float32)
        rows = rows.astype(jnp.bfloat16).reshape(peers, capacity, row_width)
        return exchange(rows).reshape(slots, row_width)

    def give_back(slot_part):
        back = exchange(slot_part.reshape(peers, capacity, row_width)).reshape(slots, row_width)
        return lax.dot_general(
            asked_pick, back, (((0,), (0,)), ((), ())), preferred_element_type=jnp.float32
        )

    wide = relay(tiles.transpose(1, 2, 0))
    rows = (jnp.arange(peers, dtype=jnp.int32)[:, None] * (fibres + NOTE_ROWS) + want_list[0]).reshape(slots)
    spread = jnp.arange(peers * (fibres + NOTE_ROWS), dtype=jnp.int32)
    first_pick = (rows[:, None] == spread[None, :]).astype(jnp.bfloat16)
    far = jnp.dot(
        first_pick, everyone.reshape(-1, row_width), preferred_element_type=jnp.float32
    ).astype(jnp.bfloat16)
    slot_part = mirror(wide, forces, mirror_own, mirror_slot, slots)
    own_part = direct(wide, far, tile_local, tile_slot, fibres)
    krylov_one = (own_part + give_back(slot_part)).astype(jnp.bfloat16)

    far = fetch(krylov_one)
    slot_part = mirror(wide, krylov_one, mirror_own, mirror_slot, slots)
    own_part = direct(wide, far, tile_local, tile_slot, fibres)
    krylov_two = (own_part + give_back(slot_part)).astype(jnp.bfloat16)
    return (krylov_one, krylov_two)


def solution(mesh):
    spec = ("groups", "row")
    in_specs = (
        P(spec, None),
        P(spec, None, None),
        P(spec),
        P(spec),
        P(spec),
        P(spec, None, None),
    )
    out_specs = (P(spec, None), P(spec, None))
    return jax.shard_map(
        per_device, mesh=mesh, in_specs=in_specs, out_specs=out_specs, check_vma=False
    )
```

```python
import functools

import jax
import jax.numpy as jnp
from jax import lax
from jax.experimental import pallas as pl
from jax.experimental.pallas import tpu as pltpu
from jax.sharding import PartitionSpec as P

NRHS = 8
LANES = 128
QUADS_PER_LOOP = 32
PAIRS_PER_CHUNK = 64
CHUNKS_HELD = 4
STRIDE_PAD = 1
RELAY_LOOPS = 4
TILE_BLOCK = 128
RELAY_VMEM = 36 * 1024 * 1024
PRODUCT_VMEM = 28 * 1024 * 1024


def in_hbm(x):
    return pltpu.with_memory_space_constraint(x, pltpu.HBM)


def fill_near(field_ref, near_ref):
    fibres, width = field_ref.shape
    unknowns = width // NRHS
    field = field_ref[...].astype(jnp.float32)
    blank = jnp.zeros((fibres, unknowns), jnp.float32)
    for r in range(NRHS):
        part = field[:, r * unknowns : (r + 1) * unknowns]
        near_ref[:fibres, r, :] = jnp.concatenate([part, blank], axis=1)
        near_ref[fibres:, r, :] = jnp.concatenate([blank, part], axis=1)


def mirror_quad(own_at, near_ref, first, halves):
    fibres = near_ref.shape[0] // 2
    left = jnp.concatenate(
        [near_ref[own_at[first + t] + fibres * (t % 2)] for t in range(4)], axis=0
    )
    right = jnp.concatenate(halves, axis=1)
    return jnp.dot(left.astype(jnp.bfloat16), right, preferred_element_type=jnp.float32)


def mirror_add(slot_at, flag_at, sum_ref, first, found):
    spare = sum_ref.shape[0] - 1
    for t in range(4):
        lane = (t // 2) * LANES
        slot = jnp.where(flag_at[first + t] == 1, slot_at[first + t], spare)
        sum_ref[slot] += found[t * NRHS : (t + 1) * NRHS, lane : lane + LANES]


def slot_rows(sum_ref, slots, unknowns):
    rows = [sum_ref[:slots, r, :][:, :unknowns] for r in range(NRHS)]
    return jnp.concatenate(rows, axis=1)


def relay_kernel(base, final, own_at, slot_at, flag_at, native_ref, field_ref, *rest):
    if final:
        _, sum_in_ref, wide_ref, slot_ref, line_ref, near_ref, sum_ref = rest
    else:
        wide_ref, sum_ref, line_ref, near_ref = rest
    step = pl.program_id(0)
    last = pl.num_programs(0) - 1
    unknowns = native_ref.shape[0]
    block = native_ref.shape[2]
    stride = block + STRIDE_PAD
    lines = unknowns * stride
    put_at = (step % 2) * lines
    take_at = ((step + 1) % 2) * lines
    blank = jnp.zeros((LANES - unknowns, block), native_ref.dtype)
    rows = unknowns // RELAY_LOOPS
    quads = block // (4 * RELAY_LOOPS)

    def turn(loop):
        for u in range(rows):
            i = loop * rows + u
            wide = jnp.concatenate([native_ref[i], blank], axis=0)
            line_ref[pl.ds(put_at + i * stride, block), :] = wide.T.astype(jnp.float32)

    def collect(loop):
        tile_at = (base + step - 1) * block
        found = []
        for u in range(quads):
            pair = (loop * quads + u) * 2
            halves = []
            for p in range(2):
                tiles = []
                for h in range(2):
                    lines_of = pl.ds(
                        take_at + 2 * (pair + p) + h, unknowns, stride=stride
                    )
                    tiles.append(line_ref[lines_of, :].astype(wide_ref.dtype))
                halves.append(jnp.concatenate(tiles, axis=0))
                wide_ref[pair + p] = halves[p]
            found.append(mirror_quad(own_at, near_ref, tile_at + 2 * pair, halves))
        for u in range(quads):
            mirror_add(slot_at, flag_at, sum_ref, tile_at + 4 * (loop * quads + u), found[u])

    def run(*parts):
        def body(loop, carry):
            for part in parts:
                part(loop)
            return carry

        lax.fori_loop(0, RELAY_LOOPS, body, 0)

    @pl.when(step == 0)
    def _():
        if final:
            sum_ref[...] = sum_in_ref[...]
        else:
            sum_ref[...] = jnp.zeros_like(sum_ref)
        fill_near(field_ref, near_ref)
        run(turn)

    @pl.when(jnp.logical_and(step > 0, step < last))
    def _():
        run(collect, turn)

    @pl.when(step == last)
    def _():
        run(collect)
        if final:
            slot_ref[...] = slot_rows(sum_ref, slot_ref.shape[0], unknowns).astype(
                slot_ref.dtype
            )


def relay_mirror(native, field, indices, slots, base, steps, earlier=None):
    unknowns, _, blocks = native.shape
    fibres, width = field.shape
    final = earlier is not None
    depth = 2 * unknowns
    sum_shape = (slots + 1, NRHS, LANES)
    in_specs = [
        pl.BlockSpec(
            (unknowns, unknowns, TILE_BLOCK),
            lambda i, *_: (0, 0, base + jnp.minimum(i, steps - 1)),
        ),
        pl.BlockSpec((fibres, width), lambda i, *_: (0, 0)),
    ]
    operands = [in_hbm(native), in_hbm(field)]
    out_shape = [pltpu.HBM((blocks // 2, depth, LANES), native.dtype)]
    out_specs = [
        pl.BlockSpec(
            (TILE_BLOCK // 2, depth, LANES), lambda i, *_: (base + jnp.maximum(i - 1, 0), 0, 0)
        )
    ]
    scratch_shapes = [
        pltpu.VMEM((2 * unknowns * (TILE_BLOCK + STRIDE_PAD), LANES), jnp.float32),
        pltpu.VMEM((2 * fibres, NRHS, depth), jnp.float32),
    ]
    if final:
        wide, sums = earlier
        in_specs += [
            pl.BlockSpec(memory_space=pltpu.HBM),
            pl.BlockSpec(sum_shape, lambda i, *_: (0, 0, 0)),
        ]
        operands += [in_hbm(wide), sums]
        out_shape.append(jax.ShapeDtypeStruct((slots, width), jnp.bfloat16))
        out_specs.append(pl.BlockSpec((slots, width), lambda i, *_: (0, 0)))
        scratch_shapes.append(pltpu.VMEM(sum_shape, jnp.float32))
    else:
        out_shape.append(jax.ShapeDtypeStruct(sum_shape, jnp.float32))
        out_specs.append(pl.BlockSpec(sum_shape, lambda i, *_: (0, 0, 0)))
    return pl.pallas_call(
        functools.partial(relay_kernel, base, final),
        out_shape=out_shape,
        grid_spec=pltpu.PrefetchScalarGridSpec(
            num_scalar_prefetch=3,
            grid=(steps + 1,),
            in_specs=in_specs,
            out_specs=out_specs,
            scratch_shapes=scratch_shapes,
        ),
        input_output_aliases={5: 0} if final else {},
        compiler_params=pltpu.CompilerParams(vmem_limit_bytes=RELAY_VMEM),
        cost_estimate=pl.CostEstimate(
            flops=4 * steps * TILE_BLOCK * unknowns * NRHS * LANES,
            bytes_accessed=8 * steps * TILE_BLOCK * unknowns * LANES,
            transcendentals=0,
        ),
        name="relay_final" if final else "relay",
    )(*[in_hbm(x) for x in indices], *operands)


def chunk_copy(tile_ref, held_ref, ready, chunk):
    slot = chunk % CHUNKS_HELD
    return pltpu.make_async_copy(
        tile_ref.at[pl.ds(chunk * PAIRS_PER_CHUNK, PAIRS_PER_CHUNK)],
        held_ref.at[slot],
        ready.at[slot],
    )


def open_stream(tile_ref, held_ref, ready):
    for chunk in range(CHUNKS_HELD - 1):
        chunk_copy(tile_ref, held_ref, ready, chunk).start()


def run_stream(tile_ref, held_ref, ready, quads):
    chunks = tile_ref.shape[0] // PAIRS_PER_CHUNK

    def body(chunk, carry):
        chunk_copy(tile_ref, held_ref, ready, chunk).wait()

        @pl.when(chunk + CHUNKS_HELD - 1 < chunks)
        def _():
            chunk_copy(tile_ref, held_ref, ready, chunk + CHUNKS_HELD - 1).start()

        held = held_ref.at[chunk % CHUNKS_HELD]

        def inner(loop, carry):
            quads(held, loop * 2 * QUADS_PER_LOOP, chunk * PAIRS_PER_CHUNK)
            return carry

        return lax.fori_loop(0, PAIRS_PER_CHUNK // (2 * QUADS_PER_LOOP), inner, carry)

    lax.fori_loop(0, chunks, body, 0)


def mirror_kernel(
    own_at, slot_at, flag_at, tile_ref, field_ref, slot_ref, held_ref, ready, near_ref, sum_ref
):
    open_stream(tile_ref, held_ref, ready)
    slots, width = slot_ref.shape
    sum_ref[...] = jnp.zeros_like(sum_ref)
    fill_near(field_ref, near_ref)

    def quads(held, pair_at, chunk_at):
        first = 2 * (chunk_at + pair_at)
        found = []
        for u in range(QUADS_PER_LOOP):
            pair = pair_at + 2 * u
            found.append(
                mirror_quad(own_at, near_ref, first + 4 * u, [held[pair], held[pair + 1]])
            )
        for u in range(QUADS_PER_LOOP):
            mirror_add(slot_at, flag_at, sum_ref, first + 4 * u, found[u])

    run_stream(tile_ref, held_ref, ready, quads)
    slot_ref[...] = slot_rows(sum_ref, slots, width // NRHS).astype(slot_ref.dtype)


def product_call(kernel, name, tiles, field, indices, out_shape, scratch_shapes):
    pairs, depth, _ = tiles.shape
    whole = pl.BlockSpec(memory_space=pltpu.VMEM)
    stay = pl.BlockSpec(memory_space=pltpu.HBM)
    stream_shapes = [
        pltpu.VMEM((CHUNKS_HELD, PAIRS_PER_CHUNK, depth, LANES), tiles.dtype),
        pltpu.SemaphoreType.DMA((CHUNKS_HELD,)),
    ]
    index = pl.BlockSpec(memory_space=pltpu.SMEM)
    return pl.pallas_call(
        kernel,
        out_shape=out_shape,
        in_specs=[index] * len(indices) + [stay, whole],
        out_specs=whole,
        scratch_shapes=stream_shapes + scratch_shapes,
        compiler_params=pltpu.CompilerParams(vmem_limit_bytes=PRODUCT_VMEM),
        cost_estimate=pl.CostEstimate(
            flops=4 * pairs * depth * NRHS * LANES,
            bytes_accessed=2 * pairs * depth * LANES,
            transcendentals=0,
        ),
        name=name,
    )(*[in_hbm(x) for x in indices], in_hbm(tiles), field)


def mirror(tiles, field, indices, slots):
    fibres, width = field.shape
    return product_call(
        mirror_kernel,
        "mirror",
        tiles,
        field,
        indices,
        jax.ShapeDtypeStruct((slots, width), jnp.bfloat16),
        [
            pltpu.VMEM((2 * fibres, NRHS, tiles.shape[1]), jnp.float32),
            pltpu.VMEM((slots + 1, NRHS, LANES), jnp.float32),
        ],
    )


def direct_kernel(
    own_at, slot_at, tile_ref, field_ref, own_ref, held_ref, ready, far_ref, even_ref, odd_ref
):
    open_stream(tile_ref, held_ref, ready)
    slots, width = field_ref.shape
    unknowns = width // NRHS
    even_ref[...] = jnp.zeros_like(even_ref)
    odd_ref[...] = jnp.zeros_like(odd_ref)
    field = field_ref[...].astype(jnp.float32)
    blank = jnp.zeros((slots, LANES - unknowns), jnp.float32)
    for r in range(NRHS):
        part = field[:, r * unknowns : (r + 1) * unknowns]
        far_ref[:, r, :] = jnp.concatenate([part, blank], axis=1)

    none = jnp.zeros((NRHS, LANES), jnp.float32)

    def quads(held, pair_at, chunk_at):
        first = 2 * (chunk_at + pair_at)
        found = []
        for u in range(QUADS_PER_LOOP):
            pair = pair_at + 2 * u
            far = [far_ref[slot_at[first + 4 * u + t]] for t in range(4)]
            left = jnp.concatenate(
                [
                    jnp.concatenate(far[:2] + [none, none], axis=0),
                    jnp.concatenate([none, none] + far[2:], axis=0),
                ],
                axis=1,
            ).astype(jnp.bfloat16)
            right = jnp.concatenate([held[pair], held[pair + 1]], axis=1)
            found.append(
                lax.dot_general(
                    left, right, (((1,), (1,)), ((), ())), preferred_element_type=jnp.float32
                )
            )
        for u in range(QUADS_PER_LOOP):
            for t in range(4):
                rows = found[u][t * NRHS : (t + 1) * NRHS]
                own = own_at[first + 4 * u + t]
                if t % 2 == 0:
                    even_ref[own] += rows[:, :LANES]
                else:
                    odd_ref[own] += rows

    run_stream(tile_ref, held_ref, ready, quads)
    rows = [
        even_ref[:, r, :][:, :unknowns] + odd_ref[:, r, :][:, unknowns:] for r in range(NRHS)
    ]
    own_ref[...] = jnp.concatenate(rows, axis=1)


def direct(tiles, field, indices, fibres):
    slots, width = field.shape
    return product_call(
        direct_kernel,
        "direct",
        tiles,
        field,
        indices,
        jax.ShapeDtypeStruct((fibres, width), jnp.float32),
        [
            pltpu.VMEM((slots, NRHS, LANES), jnp.float32),
            pltpu.VMEM((fibres, NRHS, LANES), jnp.float32),
            pltpu.VMEM((fibres, NRHS, tiles.shape[1]), jnp.float32),
        ],
    )


def per_device(forces, tiles, tile_local, tile_slot, tile_flag, want_list):
    fibres, row_width = forces.shape
    blocks = tiles.shape[0]
    _, peers, capacity = want_list.shape
    slots = peers * capacity

    def exchange(rows):
        return lax.all_to_all(rows, "row", 0, 0)

    direct_at = (tile_local, tile_slot)
    mirror_at = (tile_local, tile_slot, tile_flag)
    half = blocks // TILE_BLOCK // 2
    relay_part = functools.partial(
        relay_mirror, tiles.transpose(1, 2, 0), forces, mirror_at, slots
    )

    asked = exchange(want_list[0])
    part = relay_part(0, half)
    asked, part = lax.optimization_barrier((asked, part))
    asked = asked.reshape(slots)
    asked_pick = (asked[:, None] == jnp.arange(fibres, dtype=jnp.int32)[None, :]).astype(
        jnp.bfloat16
    )
    def fetch(current):
        rows = jnp.dot(asked_pick, current, preferred_element_type=jnp.float32)
        rows = rows.astype(jnp.bfloat16).reshape(peers, capacity, row_width)
        return exchange(rows).reshape(slots, row_width)

    def give_back(slot_part):
        back = exchange(slot_part.reshape(peers, capacity, row_width)).reshape(slots, row_width)
        return lax.dot_general(
            asked_pick, back, (((0,), (0,)), ((), ())), preferred_element_type=jnp.float32
        )

    far = fetch(forces)
    wide, slot_part = relay_part(half, blocks // TILE_BLOCK - half, part)
    own_part = direct(wide, far, direct_at, fibres)
    krylov_one = (own_part + give_back(slot_part)).astype(jnp.bfloat16)

    far = fetch(krylov_one)
    slot_part = mirror(wide, krylov_one, mirror_at, slots)
    own_part = direct(wide, far, direct_at, fibres)
    krylov_two = (own_part + give_back(slot_part)).astype(jnp.bfloat16)
    return (krylov_one, krylov_two)


def solution(mesh):
    spec = ("groups", "row")
    in_specs = (
        P(spec, None),
        P(spec, None, None),
        P(spec),
        P(spec),
        P(spec),
        P(spec, None, None),
    )
    out_specs = (P(spec, None), P(spec, None))
    return jax.shard_map(
        per_device, mesh=mesh, in_specs=in_specs, out_specs=out_specs, check_vma=False
    )
```

```python
import functools

import jax
import jax.numpy as jnp
from jax import lax
from jax.experimental import pallas as pl
from jax.experimental.pallas import tpu as pltpu
from jax.sharding import PartitionSpec as P

NRHS = 8
LANES = 128
SHARES = 3
HOSTS = SHARES + 1
CHUNKS_HELD = 3
RELAY_LOOPS = 4
STRIDE_PAD = 1
RELAY_VMEM = 52 * 1024 * 1024
PRODUCT_VMEM = 36 * 1024 * 1024
PAIRS_PER_CHUNK = LANES // 2


def in_hbm(x):
    return pltpu.with_memory_space_constraint(x, pltpu.HBM)


def tiles_of(chunk):
    group, share = chunk // SHARES, chunk % SHARES
    return share, (group * HOSTS + share) * LANES, (group * HOSTS + SHARES) * LANES


def lane_window(shape, start, stop):
    lane = lax.broadcasted_iota(jnp.int32, shape, len(shape) - 1)
    return jnp.logical_and(lane >= start, lane < stop)


def fill_near(field_ref, near_ref):
    fibres, width = field_ref.shape
    unknowns = width // NRHS
    field = field_ref[...].astype(jnp.float32)
    blank = jnp.zeros((fibres, unknowns), jnp.float32)
    for r in range(NRHS):
        part = field[:, r * unknowns : (r + 1) * unknowns]
        near_ref[:fibres, r, :] = jnp.concatenate([part, blank], axis=1)
        near_ref[fibres:, r, :] = jnp.concatenate([blank, part], axis=1)


def mirror_quad(own_at, near_ref, chunk, pair, halves):
    fibres = near_ref.shape[0] // 2
    _, host_at, guest_at = tiles_of(chunk)
    left = []
    for t in range(4):
        for first in (host_at, guest_at):
            left.append(near_ref[own_at[first + 2 * pair + t] + fibres * (t % 2)])
    left = jnp.concatenate(left, axis=0).astype(jnp.bfloat16)
    right = jnp.concatenate(halves, axis=1)
    return jnp.dot(left, right, preferred_element_type=jnp.float32)


def mirror_add(slot_at, flag_at, sums, chunk, pair, found):
    rows = sums[0].shape[0]
    share, host_at, guest_at = tiles_of(chunk)
    for t in range(4):
        lane = (t // 2) * LANES
        for m, first in enumerate((host_at, guest_at)):
            tile = first + 2 * pair + t
            slot = jnp.where(flag_at[tile] == 1, slot_at[tile], rows - 1)
            if m == 1:
                slot = slot + share * rows
            group = (2 * t + m) * NRHS
            sums[2 * m + t % 2][slot] += found[group : group + NRHS, lane : lane + LANES]


def clear(refs):
    for ref in refs:
        ref[...] = jnp.zeros_like(ref)


def write_slots(sums, slot_ref, before_ref=None):
    slots, width = slot_ref.shape
    unknowns = width // NRHS
    piece = unknowns // SHARES
    rows = sums[0].shape[0]
    step = 32

    def both(pair, at):
        total = pair[0][pl.ds(at, step)] + pair[1][pl.ds(at, step)]
        return total.reshape(step * NRHS, LANES)

    def gather(loop, carry):
        at = loop * step
        total = both(sums[:2], at)
        for share in range(SHARES):
            part = both(sums[2:], share * rows + at)
            part = pltpu.roll(part, (share * piece - unknowns) % LANES, 1)
            here = lane_window(part.shape, share * piece, (share + 1) * piece)
            total = total + jnp.where(here, part, 0.0)
        sums[0][pl.ds(at, step)] = total.reshape(step, NRHS, LANES)
        return carry

    lax.fori_loop(0, slots // step, gather, 0, unroll=2)
    parts = [sums[0][:slots, r, :][:, :unknowns] for r in range(NRHS)]
    total = jnp.concatenate(parts, axis=1)
    if before_ref is not None:
        total = total + before_ref[...]
    slot_ref[...] = total.astype(slot_ref.dtype)


def sum_scratch(slots):
    return [pltpu.VMEM((n * (slots + 1), NRHS, LANES), jnp.float32) for n in (1, 1, SHARES, SHARES)]


def relay_kernel(base, final, own_at, slot_at, flag_at, host_ref, guest_ref, field_ref, *rest):
    before_ref = rest[1] if final else None
    wide_ref, slot_ref, line_ref, near_ref, *sums = rest[2:] if final else rest
    step = pl.program_id(0)
    last = pl.num_programs(0) - 1
    unknowns = host_ref.shape[0]
    stride = LANES + STRIDE_PAD
    lines = unknowns * stride
    put_at = (step % 2) * lines
    take_at = ((step + 1) % 2) * lines
    rows = unknowns // RELAY_LOOPS
    quads = PAIRS_PER_CHUNK // (2 * RELAY_LOOPS)

    def turn(loop):
        for u in range(rows):
            i = loop * rows + u
            block = jnp.concatenate([host_ref[i], guest_ref[i]], axis=0)
            line_ref[pl.ds(put_at + i * stride, LANES), :] = block.T.astype(jnp.float32)

    def collect(loop):
        found = []
        for u in range(quads):
            pair = (loop * quads + u) * 2
            halves = []
            for p in range(2):
                tiles = []
                for h in range(2):
                    lines_of = pl.ds(take_at + 2 * (pair + p) + h, unknowns, stride=stride)
                    tiles.append(line_ref[lines_of, :].astype(wide_ref.dtype))
                halves.append(jnp.concatenate(tiles, axis=0))
                wide_ref[pair + p] = halves[p]
            found.append(mirror_quad(own_at, near_ref, base + step - 1, pair, halves))
        for u in range(quads):
            pair = (loop * quads + u) * 2
            mirror_add(slot_at, flag_at, sums, base + step - 1, pair, found[u])

    def run(*parts):
        def body(loop, carry):
            for part in parts:
                part(loop)
            return carry

        lax.fori_loop(0, RELAY_LOOPS, body, 0)

    @pl.when(step == 0)
    def _():
        clear(sums)
        fill_near(field_ref, near_ref)
        run(turn)

    @pl.when(jnp.logical_and(step > 0, step < last))
    def _():
        run(collect, turn)

    @pl.when(step == last)
    def _():
        run(collect)
        write_slots(sums, slot_ref, before_ref)


def relay_mirror(native, field, indices, slots, base, count, earlier=None):
    unknowns, _, blocks = native.shape
    fibres, width = field.shape
    depth = 2 * unknowns
    chunks = blocks // (HOSTS * LANES) * SHARES
    piece = unknowns // SHARES
    final = earlier is not None

    def host_map(i, *_):
        _, host_at, _ = tiles_of(base + jnp.minimum(i, count - 1))
        return (0, 0, host_at // LANES)

    def guest_map(i, *_):
        share, _, guest_at = tiles_of(base + jnp.minimum(i, count - 1))
        return (0, share, guest_at // LANES)

    in_specs = [
        pl.BlockSpec((unknowns, unknowns, LANES), host_map),
        pl.BlockSpec((unknowns, piece, LANES), guest_map),
        pl.BlockSpec((fibres, width), lambda i, *_: (0, 0)),
    ]
    operands = [in_hbm(x) for x in (*indices, native, native, field)]
    if final:
        in_specs.append(pl.BlockSpec(memory_space=pltpu.HBM))
        in_specs.append(pl.BlockSpec((slots, width), lambda i, *_: (0, 0)))
        operands += [in_hbm(x) for x in earlier]
    return pl.pallas_call(
        functools.partial(relay_kernel, base, final),
        out_shape=[
            pltpu.HBM((chunks * PAIRS_PER_CHUNK, depth, LANES), native.dtype),
            jax.ShapeDtypeStruct((slots, width), jnp.bfloat16 if final else jnp.float32),
        ],
        grid_spec=pltpu.PrefetchScalarGridSpec(
            num_scalar_prefetch=3,
            grid=(count + 1,),
            in_specs=in_specs,
            out_specs=[
                pl.BlockSpec(
                    (PAIRS_PER_CHUNK, depth, LANES), lambda i, *_: (base + jnp.maximum(i - 1, 0), 0, 0)
                ),
                pl.BlockSpec((slots, width), lambda i, *_: (0, 0)),
            ],
            scratch_shapes=[
                pltpu.VMEM((2 * unknowns * (LANES + STRIDE_PAD), LANES), jnp.float32),
                pltpu.VMEM((2 * fibres, NRHS, depth), jnp.float32),
            ]
            + sum_scratch(slots),
        ),
        input_output_aliases={6: 0} if final else {},
        compiler_params=pltpu.CompilerParams(vmem_limit_bytes=RELAY_VMEM),
        cost_estimate=pl.CostEstimate(
            flops=16 * count * LANES * unknowns * NRHS * LANES,
            bytes_accessed=4 * count * LANES * unknowns * LANES,
            transcendentals=0,
        ),
        name="relay_rest" if final else "relay",
    )(*operands)


def chunk_copy(tile_ref, held_ref, ready, chunk):
    slot = chunk % CHUNKS_HELD
    return pltpu.make_async_copy(
        tile_ref.at[pl.ds(chunk * PAIRS_PER_CHUNK, PAIRS_PER_CHUNK)],
        held_ref.at[slot],
        ready.at[slot],
    )


def open_stream(tile_ref, held_ref, ready):
    for chunk in range(CHUNKS_HELD - 1):
        chunk_copy(tile_ref, held_ref, ready, chunk).start()


def run_stream(tile_ref, held_ref, ready, product):
    chunks = tile_ref.shape[0] // PAIRS_PER_CHUNK

    def body(chunk, carry):
        chunk_copy(tile_ref, held_ref, ready, chunk).wait()

        @pl.when(chunk + CHUNKS_HELD - 1 < chunks)
        def _():
            chunk_copy(tile_ref, held_ref, ready, chunk + CHUNKS_HELD - 1).start()

        product(held_ref.at[chunk % CHUNKS_HELD], chunk)
        return carry

    lax.fori_loop(0, chunks, body, 0)


def mirror_kernel(
    own_at,
    slot_at,
    flag_at,
    tile_ref,
    field_ref,
    slot_ref,
    held_ref,
    ready,
    near_ref,
    *sums,
):
    open_stream(tile_ref, held_ref, ready)
    clear(sums)
    fill_near(field_ref, near_ref)

    def product(held, chunk):
        pairs = range(0, PAIRS_PER_CHUNK, 2)
        found = [
            mirror_quad(own_at, near_ref, chunk, pair, [held[pair], held[pair + 1]])
            for pair in pairs
        ]
        for pair, one in zip(pairs, found):
            mirror_add(slot_at, flag_at, sums, chunk, pair, one)

    run_stream(tile_ref, held_ref, ready, product)
    write_slots(sums, slot_ref)


def product_call(kernel, name, tiles, field, indices, out_shape, scratch_shapes):
    pairs, depth, _ = tiles.shape
    whole = pl.BlockSpec(memory_space=pltpu.VMEM)
    stay = pl.BlockSpec(memory_space=pltpu.HBM)
    stream_shapes = [
        pltpu.VMEM((CHUNKS_HELD, PAIRS_PER_CHUNK, depth, LANES), tiles.dtype),
        pltpu.SemaphoreType.DMA((CHUNKS_HELD,)),
    ]
    index = pl.BlockSpec(memory_space=pltpu.SMEM)
    return pl.pallas_call(
        kernel,
        out_shape=out_shape,
        in_specs=[index] * len(indices) + [stay, whole],
        out_specs=whole,
        scratch_shapes=stream_shapes + scratch_shapes,
        compiler_params=pltpu.CompilerParams(vmem_limit_bytes=PRODUCT_VMEM),
        cost_estimate=pl.CostEstimate(
            flops=4 * pairs * depth * NRHS * LANES,
            bytes_accessed=2 * pairs * depth * LANES,
            transcendentals=0,
        ),
        name=name,
    )(*[in_hbm(x) for x in indices], in_hbm(tiles), field)


def mirror(tiles, field, indices, slots):
    fibres, width = field.shape
    return product_call(
        mirror_kernel,
        "mirror",
        tiles,
        field,
        indices,
        jax.ShapeDtypeStruct((slots, width), jnp.bfloat16),
        [
            pltpu.VMEM((2 * fibres, NRHS, tiles.shape[1]), jnp.float32),
        ]
        + sum_scratch(slots),
    )


def fill_far(field_ref, far_ref):
    slots, width = field_ref.shape
    unknowns = width // NRHS
    piece = unknowns // SHARES
    step = 32
    field = field_ref[...].astype(jnp.float32)
    blank = jnp.zeros((slots, LANES - unknowns), jnp.float32)
    for r in range(NRHS):
        part = field[:, r * unknowns : (r + 1) * unknowns]
        far_ref[:slots, r, :] = jnp.concatenate([part, blank], axis=1)

    def spread(loop, carry):
        at = loop * step
        whole = far_ref[pl.ds(at, step)].reshape(step * NRHS, LANES)
        there = lane_window(whole.shape, unknowns, LANES)
        for share in range(SHARES):
            part = pltpu.roll(whole, (unknowns - share * piece) % LANES, 1)
            part = jnp.where(there, part, 0.0)
            far_ref[pl.ds((1 + share) * slots + at, step)] = part.reshape(step, NRHS, LANES)
        return carry

    lax.fori_loop(0, slots // step, spread, 0)


def direct_kernel(
    own_at, slot_at, tile_ref, field_ref, own_ref, held_ref, ready, far_ref, *sums
):
    open_stream(tile_ref, held_ref, ready)
    slots, width = field_ref.shape
    unknowns = width // NRHS
    clear(sums)
    fill_far(field_ref, far_ref)
    none = [jnp.zeros((NRHS, LANES), jnp.float32)] * 4

    def product(held, chunk):
        share, host_at, guest_at = tiles_of(chunk)
        pairs = range(0, PAIRS_PER_CHUNK, 2)
        found = []
        for pair in pairs:
            far = []
            for t in range(4):
                far.append(far_ref[slot_at[host_at + 2 * pair + t]])
                far.append(far_ref[slot_at[guest_at + 2 * pair + t] + (1 + share) * slots])
            left = jnp.concatenate(
                [
                    jnp.concatenate(far[:4] + none, axis=0),
                    jnp.concatenate(none + far[4:], axis=0),
                ],
                axis=1,
            ).astype(jnp.bfloat16)
            right = jnp.concatenate([held[pair], held[pair + 1]], axis=1)
            found.append(
                lax.dot_general(
                    left, right, (((1,), (1,)), ((), ())), preferred_element_type=jnp.float32
                )
            )
        for pair, one in zip(pairs, found):
            for t in range(4):
                for m, first in enumerate((host_at, guest_at)):
                    rows = one[(2 * t + m) * NRHS : (2 * t + m + 1) * NRHS]
                    own = own_at[first + 2 * pair + t]
                    if t % 2 == 0:
                        sums[m][own] += rows[:, :LANES]
                    else:
                        sums[2 + m][own] += rows

    run_stream(tile_ref, held_ref, ready, product)
    rows = [
        (sums[0][:, r, :] + sums[1][:, r, :])[:, :unknowns]
        + (sums[2][:, r, :] + sums[3][:, r, :])[:, unknowns:]
        for r in range(NRHS)
    ]
    own_ref[...] = jnp.concatenate(rows, axis=1)


def direct(tiles, field, indices, fibres):
    slots, width = field.shape
    return product_call(
        direct_kernel,
        "direct",
        tiles,
        field,
        indices,
        jax.ShapeDtypeStruct((fibres, width), jnp.float32),
        [
            pltpu.VMEM((HOSTS * slots, NRHS, LANES), jnp.float32),
            pltpu.VMEM((fibres, NRHS, LANES), jnp.float32),
            pltpu.VMEM((fibres, NRHS, LANES), jnp.float32),
            pltpu.VMEM((fibres, NRHS, tiles.shape[1]), jnp.float32),
            pltpu.VMEM((fibres, NRHS, tiles.shape[1]), jnp.float32),
        ],
    )


def per_device(forces, tiles, tile_local, tile_slot, tile_flag, want_list):
    fibres, row_width = forces.shape
    _, peers, capacity = want_list.shape
    slots = peers * capacity

    def exchange(rows):
        return lax.all_to_all(rows, "row", 0, 0, tiled=True)

    direct_at = (tile_local, tile_slot)
    mirror_at = (tile_local, tile_slot, tile_flag)
    chunks = tiles.shape[0] // (HOSTS * LANES) * SHARES
    relay_part = functools.partial(
        relay_mirror, tiles.transpose(1, 2, 0), forces, mirror_at, slots
    )

    asked = exchange(want_list[0])
    part = relay_part(0, chunks // 2)
    asked, part = lax.optimization_barrier((asked, part))
    asked = asked.reshape(slots)
    asked_pick = (asked[:, None] == jnp.arange(fibres, dtype=jnp.int32)[None, :]).astype(
        jnp.bfloat16
    )
    def fetch(current):
        rows = jnp.dot(asked_pick, current, preferred_element_type=jnp.float32)
        return exchange(rows.astype(jnp.bfloat16))

    def give_back(slot_part):
        return lax.dot_general(
            asked_pick, exchange(slot_part), (((0,), (0,)), ((), ())), preferred_element_type=jnp.float32
        )

    far = fetch(forces)
    wide, slot_part = relay_part(chunks // 2, chunks - chunks // 2, part)
    own_part = direct(wide, far, direct_at, fibres)
    krylov_one = (own_part + give_back(slot_part)).astype(jnp.bfloat16)

    far = fetch(krylov_one)
    slot_part = mirror(wide, krylov_one, mirror_at, slots)
    own_part = direct(wide, far, direct_at, fibres)
    krylov_two = (own_part + give_back(slot_part)).astype(jnp.bfloat16)
    return (krylov_one, krylov_two)


def solution(mesh):
    spec = ("groups", "row")
    in_specs = (
        P(spec, None),
        P(spec, None, None),
        P(spec),
        P(spec),
        P(spec),
        P(spec, None, None),
    )
    out_specs = (P(spec, None), P(spec, None))
    return jax.shard_map(
        per_device, mesh=mesh, in_specs=in_specs, out_specs=out_specs, check_vma=False
    )
```

```python
import functools

import jax
import jax.numpy as jnp
from jax import lax
from jax.experimental import pallas as pl
from jax.experimental.pallas import tpu as pltpu
from jax.sharding import PartitionSpec as P

NRHS = 8
LANES = 128
SHARES = 3
HOSTS = SHARES + 1
CHUNKS_HELD = 3
RELAY_LOOPS = 4
STRIDE_PAD = 1
RELAY_VMEM = 52 * 1024 * 1024
PRODUCT_VMEM = 36 * 1024 * 1024
PAIRS_PER_CHUNK = LANES // 2


def in_hbm(x):
    return pltpu.with_memory_space_constraint(x, pltpu.HBM)


def tiles_of(chunk):
    group, share = chunk // SHARES, chunk % SHARES
    return share, (group * HOSTS + share) * LANES, (group * HOSTS + SHARES) * LANES


def lane_window(shape, start, stop):
    lane = lax.broadcasted_iota(jnp.int32, shape, len(shape) - 1)
    return jnp.logical_and(lane >= start, lane < stop)


def fill_near(field_ref, near_ref):
    fibres, width = field_ref.shape
    unknowns = width // NRHS
    field = field_ref[...].astype(jnp.float32)
    blank = jnp.zeros((fibres, unknowns), jnp.float32)
    for r in range(NRHS):
        part = field[:, r * unknowns : (r + 1) * unknowns]
        near_ref[:fibres, r, :] = jnp.concatenate([part, blank], axis=1)
        near_ref[fibres:, r, :] = jnp.concatenate([blank, part], axis=1)


def mirror_quad(own_at, near_ref, chunk, pair, halves):
    fibres = near_ref.shape[0] // 2
    _, host_at, guest_at = tiles_of(chunk)
    left = []
    for t in range(4):
        for first in (host_at, guest_at):
            left.append(near_ref[own_at[first + 2 * pair + t] + fibres * (t % 2)])
    left = jnp.concatenate(left, axis=0).astype(jnp.bfloat16)
    right = jnp.concatenate(halves, axis=1)
    return jnp.dot(left, right, preferred_element_type=jnp.float32)


def mirror_add(slot_at, flag_at, sums, chunk, pair, found):
    rows = sums[0].shape[0]
    share, host_at, guest_at = tiles_of(chunk)
    for t in range(4):
        lane = (t // 2) * LANES
        for m, first in enumerate((host_at, guest_at)):
            tile = first + 2 * pair + t
            slot = jnp.where(flag_at[tile] == 1, slot_at[tile], rows - 1)
            if m == 1:
                slot = slot + share * rows
            group = (2 * t + m) * NRHS
            sums[2 * m + t % 2][slot] += found[group : group + NRHS, lane : lane + LANES]


def clear(refs):
    for ref in refs:
        ref[...] = jnp.zeros_like(ref)


def write_slots(sums, slot_ref, before_ref=None):
    slots, width = slot_ref.shape
    unknowns = width // NRHS
    piece = unknowns // SHARES
    rows = sums[0].shape[0]
    step = 32

    def both(pair, at):
        total = pair[0][pl.ds(at, step)] + pair[1][pl.ds(at, step)]
        return total.reshape(step * NRHS, LANES)

    def gather(loop, carry):
        at = loop * step
        total = both(sums[:2], at)
        for share in range(SHARES):
            part = both(sums[2:], share * rows + at)
            part = pltpu.roll(part, (share * piece - unknowns) % LANES, 1)
            here = lane_window(part.shape, share * piece, (share + 1) * piece)
            total = total + jnp.where(here, part, 0.0)
        sums[0][pl.ds(at, step)] = total.reshape(step, NRHS, LANES)
        return carry

    lax.fori_loop(0, slots // step, gather, 0, unroll=2)
    parts = [sums[0][:slots, r, :][:, :unknowns] for r in range(NRHS)]
    total = jnp.concatenate(parts, axis=1)
    if before_ref is not None:
        total = total + before_ref[...]
    slot_ref[...] = total.astype(slot_ref.dtype)


def sum_scratch(slots):
    return [pltpu.VMEM((n * (slots + 1), NRHS, LANES), jnp.float32) for n in (1, 1, SHARES, SHARES)]


def relay_kernel(base, count, final, own_at, slot_at, flag_at, native_ref, field_ref, *rest):
    if final:
        _, before_at, wide_ref, slot_ref, *rest = rest
        rest, before_ref = rest[:-1], rest[-1]
    else:
        before_at, before_ref = None, None
        wide_ref, slot_ref, *rest = rest
    if not final:
        echo_ref, *rest = rest
    host_ref, guest_ref, made_ref, near_from_ref, line_ref, near_ref, ready, *sums = rest
    unknowns = native_ref.shape[0]
    piece = unknowns // SHARES
    stride = LANES + STRIDE_PAD
    lines = unknowns * stride
    rows = unknowns // RELAY_LOOPS
    quads = PAIRS_PER_CHUNK // (2 * RELAY_LOOPS)

    def loads(n):
        share, host_at, guest_at = tiles_of(base + n)
        slot = n % 2
        return (
            pltpu.make_async_copy(
                native_ref.at[:, :, pl.ds(host_at, LANES)], host_ref.at[slot], ready.at[slot]
            ),
            pltpu.make_async_copy(
                native_ref.at[:, pl.ds(share * piece, piece), pl.ds(guest_at, LANES)],
                guest_ref.at[slot],
                ready.at[2 + slot],
            ),
        )

    def store(n):
        return pltpu.make_async_copy(
            made_ref.at[n % 2],
            wide_ref.at[pl.ds((base + n) * PAIRS_PER_CHUNK, PAIRS_PER_CHUNK)],
            ready.at[4 + n % 2],
        )

    fetch_field = pltpu.make_async_copy(field_ref, near_from_ref, ready.at[6])
    fetch_field.start()
    for n in range(min(2, count)):
        for copy in loads(n):
            copy.start()
    if final:
        fetch_before = pltpu.make_async_copy(before_at, before_ref, ready.at[7])
        fetch_before.start()
    clear(sums)
    fetch_field.wait()
    if not final:
        echo_ref[...] = near_from_ref[...]
    fill_near(near_from_ref, near_ref)

    def turn(n, loop):
        for u in range(rows):
            i = loop * rows + u
            block = jnp.concatenate([host_ref[n % 2, i], guest_ref[n % 2, i]], axis=0)
            at = (n % 2) * lines + i * stride
            line_ref[pl.ds(at, LANES), :] = block.T.astype(jnp.float32)

    def collect(n, loop):
        found = []
        for u in range(quads):
            pair = (loop * quads + u) * 2
            halves = []
            for p in range(2):
                tiles = []
                for h in range(2):
                    at = (n % 2) * lines + 2 * (pair + p) + h
                    lines_of = pl.ds(at, unknowns, stride=stride)
                    tiles.append(line_ref[lines_of, :].astype(made_ref.dtype))
                halves.append(jnp.concatenate(tiles, axis=0))
                made_ref[n % 2, pair + p] = halves[p]
            found.append(mirror_quad(own_at, near_ref, base + n, pair, halves))
        for u in range(quads):
            pair = (loop * quads + u) * 2
            mirror_add(slot_at, flag_at, sums, base + n, pair, found[u])

    for n in range(count + 1):
        if n < count:
            for copy in loads(n):
                copy.wait()
        if n >= 3:
            store(n - 3).wait()

        def body(loop, carry, n=n):
            if n >= 1:
                collect(n - 1, loop)
            if n < count:
                turn(n, loop)
            return carry

        lax.fori_loop(0, RELAY_LOOPS, body, 0)
        if n + 2 < count:
            for copy in loads(n + 2):
                copy.start()
        if n >= 1:
            store(n - 1).start()

    if final:
        fetch_before.wait()
    write_slots(sums, slot_ref, before_ref)
    for n in range(max(count - 2, 0), count):
        store(n).wait()


def relay_mirror(native, field, indices, slots, base, count, earlier=None):
    unknowns, _, blocks = native.shape
    fibres, width = field.shape
    depth = 2 * unknowns
    chunks = blocks // (HOSTS * LANES) * SHARES
    final = earlier is not None
    whole = pl.BlockSpec(memory_space=pltpu.VMEM)
    stay = pl.BlockSpec(memory_space=pltpu.HBM)
    index = pl.BlockSpec(memory_space=pltpu.SMEM)
    operands = [in_hbm(x) for x in (*indices, native, field)]
    out_shape = [pltpu.HBM((chunks * PAIRS_PER_CHUNK, depth, LANES), native.dtype)]
    if final:
        operands += [in_hbm(x) for x in earlier]
        out_shape.append(jax.ShapeDtypeStruct((slots, width), jnp.bfloat16))
    else:
        out_shape.append(jax.ShapeDtypeStruct((slots, width), jnp.float32))
        out_shape.append(pltpu.VMEM((fibres, width), field.dtype))
    scratch_shapes = [
        pltpu.VMEM((2, unknowns, unknowns, LANES), native.dtype),
        pltpu.VMEM((2, unknowns, unknowns // SHARES, LANES), native.dtype),
        pltpu.VMEM((2, PAIRS_PER_CHUNK, depth, LANES), native.dtype),
        pltpu.VMEM((fibres, width), field.dtype),
        pltpu.VMEM((2 * unknowns * (LANES + STRIDE_PAD), LANES), jnp.float32),
        pltpu.VMEM((2 * fibres, NRHS, depth), jnp.float32),
        pltpu.SemaphoreType.DMA((8,)),
    ] + sum_scratch(slots)
    if final:
        scratch_shapes.append(pltpu.VMEM((slots, width), jnp.float32))
    return pl.pallas_call(
        functools.partial(relay_kernel, base, count, final),
        out_shape=out_shape,
        in_specs=[index] * len(indices) + [stay] * (len(operands) - len(indices)),
        out_specs=[stay] + [whole] * (len(out_shape) - 1),
        scratch_shapes=scratch_shapes,
        input_output_aliases={5: 0} if final else {},
        compiler_params=pltpu.CompilerParams(vmem_limit_bytes=RELAY_VMEM),
        cost_estimate=pl.CostEstimate(
            flops=16 * count * LANES * unknowns * NRHS * LANES,
            bytes_accessed=4 * count * LANES * unknowns * LANES,
            transcendentals=0,
        ),
        name="relay_rest" if final else "relay",
    )(*operands)


def chunk_copy(tile_ref, held_ref, ready, chunk):
    slot = chunk % CHUNKS_HELD
    return pltpu.make_async_copy(
        tile_ref.at[pl.ds(chunk * PAIRS_PER_CHUNK, PAIRS_PER_CHUNK)],
        held_ref.at[slot],
        ready.at[slot],
    )


def open_stream(tile_ref, held_ref, ready):
    for chunk in range(CHUNKS_HELD - 1):
        chunk_copy(tile_ref, held_ref, ready, chunk).start()


def run_stream(tile_ref, held_ref, ready, product):
    chunks = tile_ref.shape[0] // PAIRS_PER_CHUNK

    def body(chunk, carry):
        chunk_copy(tile_ref, held_ref, ready, chunk).wait()

        @pl.when(chunk + CHUNKS_HELD - 1 < chunks)
        def _():
            chunk_copy(tile_ref, held_ref, ready, chunk + CHUNKS_HELD - 1).start()

        product(held_ref.at[chunk % CHUNKS_HELD], chunk)
        return carry

    lax.fori_loop(0, chunks, body, 0)


def mirror_kernel(
    own_at,
    slot_at,
    flag_at,
    tile_ref,
    field_ref,
    slot_ref,
    held_ref,
    ready,
    near_ref,
    *sums,
):
    open_stream(tile_ref, held_ref, ready)
    clear(sums)
    fill_near(field_ref, near_ref)

    def product(held, chunk):
        pairs = range(0, PAIRS_PER_CHUNK, 2)
        found = [
            mirror_quad(own_at, near_ref, chunk, pair, [held[pair], held[pair + 1]])
            for pair in pairs
        ]
        for pair, one in zip(pairs, found):
            mirror_add(slot_at, flag_at, sums, chunk, pair, one)

    run_stream(tile_ref, held_ref, ready, product)
    write_slots(sums, slot_ref)


def product_call(kernel, name, tiles, field, indices, out_shape, scratch_shapes):
    pairs, depth, _ = tiles.shape
    whole = pl.BlockSpec(memory_space=pltpu.VMEM)
    stay = pl.BlockSpec(memory_space=pltpu.HBM)
    stream_shapes = [
        pltpu.VMEM((CHUNKS_HELD, PAIRS_PER_CHUNK, depth, LANES), tiles.dtype),
        pltpu.SemaphoreType.DMA((CHUNKS_HELD,)),
    ]
    index = pl.BlockSpec(memory_space=pltpu.SMEM)
    return pl.pallas_call(
        kernel,
        out_shape=out_shape,
        in_specs=[index] * len(indices) + [stay, whole],
        out_specs=whole,
        scratch_shapes=stream_shapes + scratch_shapes,
        compiler_params=pltpu.CompilerParams(vmem_limit_bytes=PRODUCT_VMEM),
        cost_estimate=pl.CostEstimate(
            flops=4 * pairs * depth * NRHS * LANES,
            bytes_accessed=2 * pairs * depth * LANES,
            transcendentals=0,
        ),
        name=name,
    )(*[in_hbm(x) for x in indices], in_hbm(tiles), field)


def mirror(tiles, field, indices, slots):
    fibres, width = field.shape
    return product_call(
        mirror_kernel,
        "mirror",
        tiles,
        field,
        indices,
        jax.ShapeDtypeStruct((slots, width), jnp.bfloat16),
        [
            pltpu.VMEM((2 * fibres, NRHS, tiles.shape[1]), jnp.float32),
        ]
        + sum_scratch(slots),
    )


def fill_far(field_ref, far_ref):
    slots, width = field_ref.shape
    unknowns = width // NRHS
    piece = unknowns // SHARES
    step = 32
    field = field_ref[...].astype(jnp.float32)
    blank = jnp.zeros((slots, LANES - unknowns), jnp.float32)
    for r in range(NRHS):
        part = field[:, r * unknowns : (r + 1) * unknowns]
        far_ref[:slots, r, :] = jnp.concatenate([part, blank], axis=1)

    def spread(loop, carry):
        at = loop * step
        whole = far_ref[pl.ds(at, step)].reshape(step * NRHS, LANES)
        there = lane_window(whole.shape, unknowns, LANES)
        for share in range(SHARES):
            part = pltpu.roll(whole, (unknowns - share * piece) % LANES, 1)
            part = jnp.where(there, part, 0.0)
            far_ref[pl.ds((1 + share) * slots + at, step)] = part.reshape(step, NRHS, LANES)
        return carry

    lax.fori_loop(0, slots // step, spread, 0)


def direct_kernel(
    own_at, slot_at, tile_ref, field_ref, own_ref, held_ref, ready, far_ref, *sums
):
    open_stream(tile_ref, held_ref, ready)
    slots, width = field_ref.shape
    unknowns = width // NRHS
    clear(sums)
    fill_far(field_ref, far_ref)
    none = [jnp.zeros((NRHS, LANES), jnp.float32)] * 4

    def product(held, chunk):
        share, host_at, guest_at = tiles_of(chunk)
        pairs = range(0, PAIRS_PER_CHUNK, 2)
        found = []
        for pair in pairs:
            far = []
            for t in range(4):
                far.append(far_ref[slot_at[host_at + 2 * pair + t]])
                far.append(far_ref[slot_at[guest_at + 2 * pair + t] + (1 + share) * slots])
            left = jnp.concatenate(
                [
                    jnp.concatenate(far[:4] + none, axis=0),
                    jnp.concatenate(none + far[4:], axis=0),
                ],
                axis=1,
            ).astype(jnp.bfloat16)
            right = jnp.concatenate([held[pair], held[pair + 1]], axis=1)
            found.append(
                lax.dot_general(
                    left, right, (((1,), (1,)), ((), ())), preferred_element_type=jnp.float32
                )
            )
        for pair, one in zip(pairs, found):
            for t in range(4):
                for m, first in enumerate((host_at, guest_at)):
                    rows = one[(2 * t + m) * NRHS : (2 * t + m + 1) * NRHS]
                    own = own_at[first + 2 * pair + t]
                    if t % 2 == 0:
                        sums[m][own] += rows[:, :LANES]
                    else:
                        sums[2 + m][own] += rows

    run_stream(tile_ref, held_ref, ready, product)
    rows = [
        (sums[0][:, r, :] + sums[1][:, r, :])[:, :unknowns]
        + (sums[2][:, r, :] + sums[3][:, r, :])[:, unknowns:]
        for r in range(NRHS)
    ]
    own_ref[...] = jnp.concatenate(rows, axis=1)


def direct(tiles, field, indices, fibres):
    slots, width = field.shape
    return product_call(
        direct_kernel,
        "direct",
        tiles,
        field,
        indices,
        jax.ShapeDtypeStruct((fibres, width), jnp.float32),
        [
            pltpu.VMEM((HOSTS * slots, NRHS, LANES), jnp.float32),
            pltpu.VMEM((fibres, NRHS, LANES), jnp.float32),
            pltpu.VMEM((fibres, NRHS, LANES), jnp.float32),
            pltpu.VMEM((fibres, NRHS, tiles.shape[1]), jnp.float32),
            pltpu.VMEM((fibres, NRHS, tiles.shape[1]), jnp.float32),
        ],
    )


def per_device(forces, tiles, tile_local, tile_slot, tile_flag, want_list):
    fibres, row_width = forces.shape
    _, peers, capacity = want_list.shape
    slots = peers * capacity

    def exchange(rows):
        return lax.all_to_all(rows, "row", 0, 0, tiled=True)

    direct_at = (tile_local, tile_slot)
    mirror_at = (tile_local, tile_slot, tile_flag)
    chunks = tiles.shape[0] // (HOSTS * LANES) * SHARES
    relay_part = functools.partial(
        relay_mirror, tiles.transpose(1, 2, 0), forces, mirror_at, slots
    )

    asked = exchange(want_list[0])
    *part, echo = relay_part(0, chunks // 2)
    asked, part, echo = lax.optimization_barrier((asked, part, echo))
    asked = asked.reshape(slots)
    asked_pick = (asked[:, None] == jnp.arange(fibres, dtype=jnp.int32)[None, :]).astype(
        jnp.bfloat16
    )
    def fetch(current):
        rows = jnp.dot(asked_pick, current, preferred_element_type=jnp.float32)
        return exchange(rows.astype(jnp.bfloat16))

    def give_back(slot_part):
        return lax.dot_general(
            asked_pick, exchange(slot_part), (((0,), (0,)), ((), ())), preferred_element_type=jnp.float32
        )

    far = fetch(echo)
    wide, slot_part = relay_part(chunks // 2, chunks - chunks // 2, part)
    own_part = direct(wide, far, direct_at, fibres)
    krylov_one = (own_part + give_back(slot_part)).astype(jnp.bfloat16)

    far = fetch(krylov_one)
    slot_part = mirror(wide, krylov_one, mirror_at, slots)
    own_part = direct(wide, far, direct_at, fibres)
    krylov_two = (own_part + give_back(slot_part)).astype(jnp.bfloat16)
    return (krylov_one, krylov_two)


def solution(mesh):
    spec = ("groups", "row")
    in_specs = (
        P(spec, None),
        P(spec, None, None),
        P(spec),
        P(spec),
        P(spec),
        P(spec, None, None),
    )
    out_specs = (P(spec, None), P(spec, None))
    return jax.shard_map(
        per_device, mesh=mesh, in_specs=in_specs, out_specs=out_specs, check_vma=False
    )
```

```python
import functools

import jax
import jax.numpy as jnp
from jax import lax
from jax.experimental import pallas as pl
from jax.experimental.pallas import tpu as pltpu
from jax.sharding import PartitionSpec as P

NRHS = 8
LANES = 128
SHARES = 3
HOSTS = SHARES + 1
CHUNKS_HELD = 3
RELAY_LOOPS = 4
STRIDE_PAD = 1
RELAY_VMEM = 52 * 1024 * 1024
PRODUCT_VMEM = 36 * 1024 * 1024
PAIRS_PER_CHUNK = LANES // 2


def in_hbm(x):
    return pltpu.with_memory_space_constraint(x, pltpu.HBM)


def tiles_of(chunk):
    group, share = chunk // SHARES, chunk % SHARES
    return share, (group * HOSTS + share) * LANES, (group * HOSTS + SHARES) * LANES


def lane_window(shape, start, stop):
    lane = lax.broadcasted_iota(jnp.int32, shape, len(shape) - 1)
    return jnp.logical_and(lane >= start, lane < stop)


def fill_near(field_ref, near_ref):
    fibres, width = field_ref.shape
    unknowns = width // NRHS
    field = field_ref[...].astype(jnp.float32)
    blank = jnp.zeros((fibres, unknowns), jnp.float32)
    for r in range(NRHS):
        part = field[:, r * unknowns : (r + 1) * unknowns]
        near_ref[:fibres, r, :] = jnp.concatenate([part, blank], axis=1)
        near_ref[fibres:, r, :] = jnp.concatenate([blank, part], axis=1)


def mirror_quad(own_at, near_ref, chunk, pair, halves):
    fibres = near_ref.shape[0] // 2
    _, host_at, guest_at = tiles_of(chunk)
    left = []
    for t in range(4):
        for first in (host_at, guest_at):
            left.append(near_ref[own_at[first + 2 * pair + t] + fibres * (t % 2)])
    left = jnp.concatenate(left, axis=0).astype(jnp.bfloat16)
    right = jnp.concatenate(halves, axis=1)
    return jnp.dot(left, right, preferred_element_type=jnp.float32)


def mirror_add(slot_at, flag_at, sums, chunk, pair, found):
    rows = sums[0].shape[0]
    share, host_at, guest_at = tiles_of(chunk)
    for t in range(4):
        lane = (t // 2) * LANES
        for m, first in enumerate((host_at, guest_at)):
            tile = first + 2 * pair + t
            slot = jnp.where(flag_at[tile] == 1, slot_at[tile], rows - 1)
            if m == 1:
                slot = slot + share * rows
            group = (2 * t + m) * NRHS
            sums[2 * m + t % 2][slot] += found[group : group + NRHS, lane : lane + LANES]


def clear(refs):
    for ref in refs:
        ref[...] = jnp.zeros_like(ref)


def write_slots(sums, slot_ref, before_ref=None):
    slots, width = slot_ref.shape
    unknowns = width // NRHS
    piece = unknowns // SHARES
    rows = sums[0].shape[0]
    step = 32

    def both(pair, at):
        total = pair[0][pl.ds(at, step)] + pair[1][pl.ds(at, step)]
        return total.reshape(step * NRHS, LANES)

    def gather(loop, carry):
        at = loop * step
        total = both(sums[:2], at)
        for share in range(SHARES):
            part = both(sums[2:], share * rows + at)
            part = pltpu.roll(part, (share * piece - unknowns) % LANES, 1)
            here = lane_window(part.shape, share * piece, (share + 1) * piece)
            total = total + jnp.where(here, part, 0.0)
        sums[0][pl.ds(at, step)] = total.reshape(step, NRHS, LANES)
        return carry

    lax.fori_loop(0, slots // step, gather, 0, unroll=2)
    parts = [sums[0][:slots, r, :][:, :unknowns] for r in range(NRHS)]
    total = jnp.concatenate(parts, axis=1)
    if before_ref is not None:
        total = total + before_ref[...]
    slot_ref[...] = total.astype(slot_ref.dtype)


def sum_scratch(slots):
    return [pltpu.VMEM((n * (slots + 1), NRHS, LANES), jnp.float32) for n in (1, 1, SHARES, SHARES)]


def relay_kernel(base, count, final, own_at, slot_at, flag_at, native_ref, field_ref, *rest):
    if final:
        _, before_ref, wide_ref, slot_ref, *rest = rest
    else:
        before_ref = None
        wide_ref, slot_ref, echo_ref, *rest = rest
    host_ref, guest_ref, made_ref, near_from_ref, line_ref, near_ref, ready, *sums = rest
    unknowns = native_ref.shape[0]
    piece = unknowns // SHARES
    stride = LANES + STRIDE_PAD
    lines = unknowns * stride
    rows = unknowns // RELAY_LOOPS
    quads = PAIRS_PER_CHUNK // (2 * RELAY_LOOPS)

    def loads(n):
        share, host_at, guest_at = tiles_of(base + n)
        slot = n % 2
        return (
            pltpu.make_async_copy(
                native_ref.at[:, :, pl.ds(host_at, LANES)], host_ref.at[slot], ready.at[slot]
            ),
            pltpu.make_async_copy(
                native_ref.at[:, pl.ds(share * piece, piece), pl.ds(guest_at, LANES)],
                guest_ref.at[slot],
                ready.at[2 + slot],
            ),
        )

    def store(n):
        return pltpu.make_async_copy(
            made_ref.at[n % 2],
            wide_ref.at[pl.ds((base + n) * PAIRS_PER_CHUNK, PAIRS_PER_CHUNK)],
            ready.at[4 + n % 2],
        )

    fetch_field = pltpu.make_async_copy(field_ref, near_from_ref, ready.at[6])
    fetch_field.start()
    for n in range(min(2, count)):
        for copy in loads(n):
            copy.start()
    clear(sums)
    fetch_field.wait()
    if not final:
        echo_ref[...] = near_from_ref[...]
    fill_near(near_from_ref, near_ref)

    def turn(n, loop):
        for u in range(rows):
            i = loop * rows + u
            block = jnp.concatenate([host_ref[n % 2, i], guest_ref[n % 2, i]], axis=0)
            at = (n % 2) * lines + i * stride
            line_ref[pl.ds(at, LANES), :] = block.T.astype(jnp.float32)

    def collect(n, loop):
        found = []
        for u in range(quads):
            pair = (loop * quads + u) * 2
            halves = []
            for p in range(2):
                tiles = []
                for h in range(2):
                    at = (n % 2) * lines + 2 * (pair + p) + h
                    lines_of = pl.ds(at, unknowns, stride=stride)
                    tiles.append(line_ref[lines_of, :].astype(made_ref.dtype))
                halves.append(jnp.concatenate(tiles, axis=0))
                made_ref[n % 2, pair + p] = halves[p]
            found.append(mirror_quad(own_at, near_ref, base + n, pair, halves))
        for u in range(quads):
            pair = (loop * quads + u) * 2
            mirror_add(slot_at, flag_at, sums, base + n, pair, found[u])

    for n in range(count + 1):
        if n < count:
            for copy in loads(n):
                copy.wait()
        if n >= 3:
            store(n - 3).wait()

        def body(loop, carry, n=n):
            if n >= 1:
                collect(n - 1, loop)
            if n < count:
                turn(n, loop)
            return carry

        lax.fori_loop(0, RELAY_LOOPS, body, 0)
        if n + 2 < count:
            for copy in loads(n + 2):
                copy.start()
        if n >= 1:
            store(n - 1).start()

    write_slots(sums, slot_ref, before_ref)
    for n in range(max(count - 2, 0), count):
        store(n).wait()


def relay_mirror(native, field, indices, slots, base, count, earlier=None):
    unknowns, _, blocks = native.shape
    fibres, width = field.shape
    depth = 2 * unknowns
    chunks = blocks // (HOSTS * LANES) * SHARES
    final = earlier is not None
    whole = pl.BlockSpec(memory_space=pltpu.VMEM)
    stay = pl.BlockSpec(memory_space=pltpu.HBM)
    index = pl.BlockSpec(memory_space=pltpu.SMEM)
    operands = [in_hbm(x) for x in (*indices, native, field)]
    in_specs = [index] * len(indices) + [stay, stay]
    out_shape = [pltpu.HBM((chunks * PAIRS_PER_CHUNK, depth, LANES), native.dtype)]
    if final:
        wide, before = earlier
        operands += [in_hbm(wide), before]
        in_specs += [stay, whole]
        out_shape.append(jax.ShapeDtypeStruct((slots, width), jnp.bfloat16))
    else:
        out_shape.append(jax.ShapeDtypeStruct((slots, width), jnp.float32))
        out_shape.append(pltpu.VMEM((fibres, width), field.dtype))
    scratch_shapes = [
        pltpu.VMEM((2, unknowns, unknowns, LANES), native.dtype),
        pltpu.VMEM((2, unknowns, unknowns // SHARES, LANES), native.dtype),
        pltpu.VMEM((2, PAIRS_PER_CHUNK, depth, LANES), native.dtype),
        pltpu.VMEM((fibres, width), field.dtype),
        pltpu.VMEM((2 * unknowns * (LANES + STRIDE_PAD), LANES), jnp.float32),
        pltpu.VMEM((2 * fibres, NRHS, depth), jnp.float32),
        pltpu.SemaphoreType.DMA((7,)),
    ] + sum_scratch(slots)
    return pl.pallas_call(
        functools.partial(relay_kernel, base, count, final),
        out_shape=out_shape,
        in_specs=in_specs,
        out_specs=[stay] + [whole] * (len(out_shape) - 1),
        scratch_shapes=scratch_shapes,
        input_output_aliases={5: 0} if final else {},
        compiler_params=pltpu.CompilerParams(vmem_limit_bytes=RELAY_VMEM),
        cost_estimate=pl.CostEstimate(
            flops=16 * count * LANES * unknowns * NRHS * LANES,
            bytes_accessed=4 * count * LANES * unknowns * LANES,
            transcendentals=0,
        ),
        name="relay_rest" if final else "relay",
    )(*operands)


def chunk_copy(tile_ref, held_ref, ready, chunk):
    slot = chunk % CHUNKS_HELD
    return pltpu.make_async_copy(
        tile_ref.at[pl.ds(chunk * PAIRS_PER_CHUNK, PAIRS_PER_CHUNK)],
        held_ref.at[slot],
        ready.at[slot],
    )


def open_stream(tile_ref, held_ref, ready):
    for chunk in range(CHUNKS_HELD - 1):
        chunk_copy(tile_ref, held_ref, ready, chunk).start()


def run_stream(tile_ref, held_ref, ready, product):
    chunks = tile_ref.shape[0] // PAIRS_PER_CHUNK

    def body(chunk, carry):
        chunk_copy(tile_ref, held_ref, ready, chunk).wait()

        @pl.when(chunk + CHUNKS_HELD - 1 < chunks)
        def _():
            chunk_copy(tile_ref, held_ref, ready, chunk + CHUNKS_HELD - 1).start()

        product(held_ref.at[chunk % CHUNKS_HELD], chunk)
        return carry

    lax.fori_loop(0, chunks, body, 0)


def mirror_kernel(
    own_at,
    slot_at,
    flag_at,
    tile_ref,
    field_ref,
    slot_ref,
    held_ref,
    ready,
    near_ref,
    *sums,
):
    open_stream(tile_ref, held_ref, ready)
    clear(sums)
    fill_near(field_ref, near_ref)

    def product(held, chunk):
        pairs = range(0, PAIRS_PER_CHUNK, 2)
        found = [
            mirror_quad(own_at, near_ref, chunk, pair, [held[pair], held[pair + 1]])
            for pair in pairs
        ]
        for pair, one in zip(pairs, found):
            mirror_add(slot_at, flag_at, sums, chunk, pair, one)

    run_stream(tile_ref, held_ref, ready, product)
    write_slots(sums, slot_ref)


def product_call(kernel, name, tiles, field, indices, out_shape, scratch_shapes):
    pairs, depth, _ = tiles.shape
    whole = pl.BlockSpec(memory_space=pltpu.VMEM)
    stay = pl.BlockSpec(memory_space=pltpu.HBM)
    stream_shapes = [
        pltpu.VMEM((CHUNKS_HELD, PAIRS_PER_CHUNK, depth, LANES), tiles.dtype),
        pltpu.SemaphoreType.DMA((CHUNKS_HELD,)),
    ]
    index = pl.BlockSpec(memory_space=pltpu.SMEM)
    return pl.pallas_call(
        kernel,
        out_shape=out_shape,
        in_specs=[index] * len(indices) + [stay, whole],
        out_specs=whole,
        scratch_shapes=stream_shapes + scratch_shapes,
        compiler_params=pltpu.CompilerParams(vmem_limit_bytes=PRODUCT_VMEM),
        cost_estimate=pl.CostEstimate(
            flops=4 * pairs * depth * NRHS * LANES,
            bytes_accessed=2 * pairs * depth * LANES,
            transcendentals=0,
        ),
        name=name,
    )(*[in_hbm(x) for x in indices], in_hbm(tiles), field)


def mirror(tiles, field, indices, slots):
    fibres, width = field.shape
    return product_call(
        mirror_kernel,
        "mirror",
        tiles,
        field,
        indices,
        jax.ShapeDtypeStruct((slots, width), jnp.bfloat16),
        [
            pltpu.VMEM((2 * fibres, NRHS, tiles.shape[1]), jnp.float32),
        ]
        + sum_scratch(slots),
    )


def fill_far(field_ref, far_ref):
    slots, width = field_ref.shape
    unknowns = width // NRHS
    piece = unknowns // SHARES
    step = 32
    field = field_ref[...].astype(jnp.float32)
    blank = jnp.zeros((slots, LANES - unknowns), jnp.float32)
    for r in range(NRHS):
        part = field[:, r * unknowns : (r + 1) * unknowns]
        far_ref[:slots, r, :] = jnp.concatenate([part, blank], axis=1)

    def spread(loop, carry):
        at = loop * step
        whole = far_ref[pl.ds(at, step)].reshape(step * NRHS, LANES)
        there = lane_window(whole.shape, unknowns, LANES)
        for share in range(SHARES):
            part = pltpu.roll(whole, (unknowns - share * piece) % LANES, 1)
            part = jnp.where(there, part, 0.0)
            far_ref[pl.ds((1 + share) * slots + at, step)] = part.reshape(step, NRHS, LANES)
        return carry

    lax.fori_loop(0, slots // step, spread, 0)


def direct_kernel(
    own_at, slot_at, tile_ref, field_ref, own_ref, held_ref, ready, far_ref, *sums
):
    open_stream(tile_ref, held_ref, ready)
    slots, width = field_ref.shape
    unknowns = width // NRHS
    clear(sums)
    fill_far(field_ref, far_ref)
    none = [jnp.zeros((NRHS, LANES), jnp.float32)] * 4

    def product(held, chunk):
        share, host_at, guest_at = tiles_of(chunk)
        pairs = range(0, PAIRS_PER_CHUNK, 2)
        found = []
        for pair in pairs:
            far = []
            for t in range(4):
                far.append(far_ref[slot_at[host_at + 2 * pair + t]])
                far.append(far_ref[slot_at[guest_at + 2 * pair + t] + (1 + share) * slots])
            left = jnp.concatenate(
                [
                    jnp.concatenate(far[:4] + none, axis=0),
                    jnp.concatenate(none + far[4:], axis=0),
                ],
                axis=1,
            ).astype(jnp.bfloat16)
            right = jnp.concatenate([held[pair], held[pair + 1]], axis=1)
            found.append(
                lax.dot_general(
                    left, right, (((1,), (1,)), ((), ())), preferred_element_type=jnp.float32
                )
            )
        for pair, one in zip(pairs, found):
            for t in range(4):
                for m, first in enumerate((host_at, guest_at)):
                    rows = one[(2 * t + m) * NRHS : (2 * t + m + 1) * NRHS]
                    own = own_at[first + 2 * pair + t]
                    if t % 2 == 0:
                        sums[m][own] += rows[:, :LANES]
                    else:
                        sums[2 + m][own] += rows

    run_stream(tile_ref, held_ref, ready, product)
    rows = [
        (sums[0][:, r, :] + sums[1][:, r, :])[:, :unknowns]
        + (sums[2][:, r, :] + sums[3][:, r, :])[:, unknowns:]
        for r in range(NRHS)
    ]
    own_ref[...] = jnp.concatenate(rows, axis=1)


def direct(tiles, field, indices, fibres):
    slots, width = field.shape
    return product_call(
        direct_kernel,
        "direct",
        tiles,
        field,
        indices,
        jax.ShapeDtypeStruct((fibres, width), jnp.float32),
        [
            pltpu.VMEM((HOSTS * slots, NRHS, LANES), jnp.float32),
            pltpu.VMEM((fibres, NRHS, LANES), jnp.float32),
            pltpu.VMEM((fibres, NRHS, LANES), jnp.float32),
            pltpu.VMEM((fibres, NRHS, tiles.shape[1]), jnp.float32),
            pltpu.VMEM((fibres, NRHS, tiles.shape[1]), jnp.float32),
        ],
    )


def per_device(forces, tiles, tile_local, tile_slot, tile_flag, want_list):
    fibres, row_width = forces.shape
    _, peers, capacity = want_list.shape
    slots = peers * capacity

    def exchange(rows):
        return lax.all_to_all(rows, "row", 0, 0, tiled=True)

    direct_at = (tile_local, tile_slot)
    mirror_at = (tile_local, tile_slot, tile_flag)
    chunks = tiles.shape[0] // (HOSTS * LANES) * SHARES
    relay_part = functools.partial(
        relay_mirror, tiles.transpose(1, 2, 0), forces, mirror_at, slots
    )

    asked = exchange(want_list[0])
    *part, echo = relay_part(0, chunks // 2)
    asked, part, echo = lax.optimization_barrier((asked, part, echo))
    asked = asked.reshape(slots)
    asked_pick = (asked[:, None] == jnp.arange(fibres, dtype=jnp.int32)[None, :]).astype(
        jnp.bfloat16
    )
    def fetch(current):
        rows = jnp.dot(asked_pick, current, preferred_element_type=jnp.float32)
        return exchange(rows.astype(jnp.bfloat16))

    def give_back(slot_part):
        return lax.dot_general(
            asked_pick, exchange(slot_part), (((0,), (0,)), ((), ())), preferred_element_type=jnp.float32
        )

    far = fetch(echo)
    wide, slot_part = relay_part(chunks // 2, chunks - chunks // 2, part)
    own_part = direct(wide, far, direct_at, fibres)
    krylov_one = (own_part + give_back(slot_part)).astype(jnp.bfloat16)

    far = fetch(krylov_one)
    slot_part = mirror(wide, krylov_one, mirror_at, slots)
    own_part = direct(wide, far, direct_at, fibres)
    krylov_two = (own_part + give_back(slot_part)).astype(jnp.bfloat16)
    return (krylov_one, krylov_two)


def solution(mesh):
    spec = ("groups", "row")
    in_specs = (
        P(spec, None),
        P(spec, None, None),
        P(spec),
        P(spec),
        P(spec),
        P(spec, None, None),
    )
    out_specs = (P(spec, None), P(spec, None))
    return jax.shard_map(
        per_device, mesh=mesh, in_specs=in_specs, out_specs=out_specs, check_vma=False
    )
```

```python
import functools

import jax
import jax.numpy as jnp
from jax import lax
from jax.experimental import pallas as pl
from jax.experimental.pallas import tpu as pltpu
from jax.sharding import PartitionSpec as P

NRHS = 8
LANES = 128
SHARES = 3
HOSTS = SHARES + 1
CHUNKS_HELD = 4
RELAY_LOOPS = 4
STRIDE_PAD = 1
RELAY_VMEM = 52 * 1024 * 1024
PRODUCT_VMEM = 36 * 1024 * 1024
PAIRS_PER_CHUNK = LANES // 2


def in_hbm(x):
    return pltpu.with_memory_space_constraint(x, pltpu.HBM)


def tiles_of(chunk):
    group, share = chunk // SHARES, chunk % SHARES
    return share, (group * HOSTS + share) * LANES, (group * HOSTS + SHARES) * LANES


def lane_window(shape, start, stop):
    lane = lax.broadcasted_iota(jnp.int32, shape, len(shape) - 1)
    return jnp.logical_and(lane >= start, lane < stop)


def fill_near(field_ref, near_ref):
    fibres, width = field_ref.shape
    unknowns = width // NRHS
    field = field_ref[...].astype(jnp.float32)
    blank = jnp.zeros((fibres, unknowns), jnp.float32)
    for r in range(NRHS):
        part = field[:, r * unknowns : (r + 1) * unknowns]
        near_ref[:fibres, r, :] = jnp.concatenate([part, blank], axis=1)
        near_ref[fibres:, r, :] = jnp.concatenate([blank, part], axis=1)


def mirror_quad(own_at, near_ref, chunk, pair, halves):
    fibres = near_ref.shape[0] // 2
    _, host_at, guest_at = tiles_of(chunk)
    left = []
    for t in range(4):
        for first in (host_at, guest_at):
            left.append(near_ref[own_at[first + 2 * pair + t] + fibres * (t % 2)])
    left = jnp.concatenate(left, axis=0).astype(jnp.bfloat16)
    right = jnp.concatenate(halves, axis=1)
    return jnp.dot(left, right, preferred_element_type=jnp.float32)


def mirror_add(slot_at, flag_at, sums, chunk, pair, found):
    rows = sums[0].shape[0]
    share, host_at, guest_at = tiles_of(chunk)
    for t in range(4):
        lane = (t // 2) * LANES
        for m, first in enumerate((host_at, guest_at)):
            tile = first + 2 * pair + t
            slot = jnp.where(flag_at[tile] == 1, slot_at[tile], rows - 1)
            if m == 1:
                slot = slot + share * rows
            group = (2 * t + m) * NRHS
            sums[2 * m + t % 2][slot] += found[group : group + NRHS, lane : lane + LANES]


def clear(refs):
    for ref in refs:
        ref[...] = jnp.zeros_like(ref)


def write_slots(sums, slot_ref, before_ref=None):
    slots, width = slot_ref.shape
    unknowns = width // NRHS
    piece = unknowns // SHARES
    rows = sums[0].shape[0]
    step = 64

    def both(pair, at):
        total = pair[0][pl.ds(at, step)] + pair[1][pl.ds(at, step)]
        return total.reshape(step * NRHS, LANES)

    def gather(loop, carry):
        at = loop * step
        total = both(sums[:2], at)
        for share in range(SHARES):
            part = both(sums[2:], share * rows + at)
            part = pltpu.roll(part, (share * piece - unknowns) % LANES, 1)
            here = lane_window(part.shape, share * piece, (share + 1) * piece)
            total = total + jnp.where(here, part, 0.0)
        sums[0][pl.ds(at, step)] = total.reshape(step, NRHS, LANES)
        return carry

    lax.fori_loop(0, slots // step, gather, 0, unroll=2)
    parts = [sums[0][:slots, r, :][:, :unknowns] for r in range(NRHS)]
    total = jnp.concatenate(parts, axis=1)
    if before_ref is not None:
        total = total + before_ref[...]
    slot_ref[...] = total.astype(slot_ref.dtype)


def sum_scratch(slots):
    return [pltpu.VMEM((n * (slots + 1), NRHS, LANES), jnp.float32) for n in (1, 1, SHARES, SHARES)]


def relay_kernel(base, count, final, own_at, slot_at, flag_at, native_ref, field_ref, *rest):
    if final:
        _, before_ref, wide_ref, slot_ref, *rest = rest
    else:
        before_ref = None
        wide_ref, slot_ref, echo_ref, *rest = rest
    host_ref, guest_ref, made_ref, near_from_ref, line_ref, near_ref, ready, *sums = rest
    unknowns = native_ref.shape[0]
    piece = unknowns // SHARES
    stride = LANES + STRIDE_PAD
    lines = unknowns * stride
    rows = unknowns // RELAY_LOOPS
    quads = PAIRS_PER_CHUNK // (2 * RELAY_LOOPS)

    def loads(n):
        share, host_at, guest_at = tiles_of(base + n)
        slot = n % 2
        return (
            pltpu.make_async_copy(
                native_ref.at[:, :, pl.ds(host_at, LANES)], host_ref.at[slot], ready.at[slot]
            ),
            pltpu.make_async_copy(
                native_ref.at[:, pl.ds(share * piece, piece), pl.ds(guest_at, LANES)],
                guest_ref.at[slot],
                ready.at[2 + slot],
            ),
        )

    def store(n):
        return pltpu.make_async_copy(
            made_ref.at[n % 2],
            wide_ref.at[pl.ds((base + n) * PAIRS_PER_CHUNK, PAIRS_PER_CHUNK)],
            ready.at[4 + n % 2],
        )

    fetch_field = pltpu.make_async_copy(field_ref, near_from_ref, ready.at[6])
    fetch_field.start()
    for n in range(min(2, count)):
        for copy in loads(n):
            copy.start()
    clear(sums)
    fetch_field.wait()
    if not final:
        echo_ref[...] = near_from_ref[...]
    fill_near(near_from_ref, near_ref)

    def turn(n, loop):
        for u in range(rows):
            i = loop * rows + u
            block = jnp.concatenate([host_ref[n % 2, i], guest_ref[n % 2, i]], axis=0)
            at = (n % 2) * lines + i * stride
            line_ref[pl.ds(at, LANES), :] = block.T.astype(jnp.float32)

    def collect(n, loop):
        found = []
        for u in range(quads):
            pair = (loop * quads + u) * 2
            halves = []
            for p in range(2):
                tiles = []
                for h in range(2):
                    at = (n % 2) * lines + 2 * (pair + p) + h
                    lines_of = pl.ds(at, unknowns, stride=stride)
                    tiles.append(line_ref[lines_of, :].astype(made_ref.dtype))
                halves.append(jnp.concatenate(tiles, axis=0))
                made_ref[n % 2, pair + p] = halves[p]
            found.append(mirror_quad(own_at, near_ref, base + n, pair, halves))
        for u in range(quads):
            pair = (loop * quads + u) * 2
            mirror_add(slot_at, flag_at, sums, base + n, pair, found[u])

    for n in range(count + 1):
        if n < count:
            for copy in loads(n):
                copy.wait()
        if n >= 3:
            store(n - 3).wait()

        def body(loop, carry, n=n):
            if n >= 1:
                collect(n - 1, loop)
            if n < count:
                turn(n, loop)
            return carry

        lax.fori_loop(0, RELAY_LOOPS, body, 0)
        if n + 2 < count:
            for copy in loads(n + 2):
                copy.start()
        if n >= 1:
            store(n - 1).start()

    write_slots(sums, slot_ref, before_ref)
    for n in range(max(count - 2, 0), count):
        store(n).wait()


def relay_mirror(native, field, indices, slots, base, count, earlier=None):
    unknowns, _, blocks = native.shape
    fibres, width = field.shape
    depth = 2 * unknowns
    chunks = blocks // (HOSTS * LANES) * SHARES
    final = earlier is not None
    whole = pl.BlockSpec(memory_space=pltpu.VMEM)
    stay = pl.BlockSpec(memory_space=pltpu.HBM)
    index = pl.BlockSpec(memory_space=pltpu.SMEM)
    operands = [in_hbm(x) for x in (*indices, native, field)]
    in_specs = [index] * len(indices) + [stay, stay]
    out_shape = [pltpu.HBM((chunks * PAIRS_PER_CHUNK, depth, LANES), native.dtype)]
    if final:
        wide, before = earlier
        operands += [in_hbm(wide), before]
        in_specs += [stay, whole]
        out_shape.append(jax.ShapeDtypeStruct((slots, width), jnp.bfloat16))
    else:
        out_shape.append(jax.ShapeDtypeStruct((slots, width), jnp.float32))
        out_shape.append(pltpu.VMEM((fibres, width), field.dtype))
    scratch_shapes = [
        pltpu.VMEM((2, unknowns, unknowns, LANES), native.dtype),
        pltpu.VMEM((2, unknowns, unknowns // SHARES, LANES), native.dtype),
        pltpu.VMEM((2, PAIRS_PER_CHUNK, depth, LANES), native.dtype),
        pltpu.VMEM((fibres, width), field.dtype),
        pltpu.VMEM((2 * unknowns * (LANES + STRIDE_PAD), LANES), jnp.float32),
        pltpu.VMEM((2 * fibres, NRHS, depth), jnp.float32),
        pltpu.SemaphoreType.DMA((7,)),
    ] + sum_scratch(slots)
    return pl.pallas_call(
        functools.partial(relay_kernel, base, count, final),
        out_shape=out_shape,
        in_specs=in_specs,
        out_specs=[stay] + [whole] * (len(out_shape) - 1),
        scratch_shapes=scratch_shapes,
        input_output_aliases={5: 0} if final else {},
        compiler_params=pltpu.CompilerParams(vmem_limit_bytes=RELAY_VMEM),
        cost_estimate=pl.CostEstimate(
            flops=16 * count * LANES * unknowns * NRHS * LANES,
            bytes_accessed=4 * count * LANES * unknowns * LANES,
            transcendentals=0,
        ),
        name="relay_rest" if final else "relay",
    )(*operands)


def chunk_copy(tile_ref, held_ref, ready, chunk):
    slot = chunk % CHUNKS_HELD
    return pltpu.make_async_copy(
        tile_ref.at[pl.ds(chunk * PAIRS_PER_CHUNK, PAIRS_PER_CHUNK)],
        held_ref.at[slot],
        ready.at[slot],
    )


def open_stream(tile_ref, held_ref, ready):
    for chunk in range(CHUNKS_HELD - 1):
        chunk_copy(tile_ref, held_ref, ready, chunk).start()


def run_stream(tile_ref, held_ref, ready, product):
    chunks = tile_ref.shape[0] // PAIRS_PER_CHUNK

    def body(chunk, carry):
        chunk_copy(tile_ref, held_ref, ready, chunk).wait()

        @pl.when(chunk + CHUNKS_HELD - 1 < chunks)
        def _():
            chunk_copy(tile_ref, held_ref, ready, chunk + CHUNKS_HELD - 1).start()

        product(held_ref.at[chunk % CHUNKS_HELD], chunk)
        return carry

    lax.fori_loop(0, chunks, body, 0)


def mirror_kernel(
    own_at,
    slot_at,
    flag_at,
    tile_ref,
    field_ref,
    slot_ref,
    held_ref,
    ready,
    near_ref,
    *sums,
):
    open_stream(tile_ref, held_ref, ready)
    clear(sums)
    fill_near(field_ref, near_ref)

    def product(held, chunk):
        pairs = range(0, PAIRS_PER_CHUNK, 2)
        found = [
            mirror_quad(own_at, near_ref, chunk, pair, [held[pair], held[pair + 1]])
            for pair in pairs
        ]
        for pair, one in zip(pairs, found):
            mirror_add(slot_at, flag_at, sums, chunk, pair, one)

    run_stream(tile_ref, held_ref, ready, product)
    write_slots(sums, slot_ref)


def product_call(kernel, name, tiles, field, indices, out_shape, scratch_shapes):
    pairs, depth, _ = tiles.shape
    whole = pl.BlockSpec(memory_space=pltpu.VMEM)
    stay = pl.BlockSpec(memory_space=pltpu.HBM)
    stream_shapes = [
        pltpu.VMEM((CHUNKS_HELD, PAIRS_PER_CHUNK, depth, LANES), tiles.dtype),
        pltpu.SemaphoreType.DMA((CHUNKS_HELD,)),
    ]
    index = pl.BlockSpec(memory_space=pltpu.SMEM)
    return pl.pallas_call(
        kernel,
        out_shape=out_shape,
        in_specs=[index] * len(indices) + [stay, whole],
        out_specs=whole,
        scratch_shapes=stream_shapes + scratch_shapes,
        compiler_params=pltpu.CompilerParams(vmem_limit_bytes=PRODUCT_VMEM),
        cost_estimate=pl.CostEstimate(
            flops=4 * pairs * depth * NRHS * LANES,
            bytes_accessed=2 * pairs * depth * LANES,
            transcendentals=0,
        ),
        name=name,
    )(*[in_hbm(x) for x in indices], in_hbm(tiles), field)


def mirror(tiles, field, indices, slots):
    fibres, width = field.shape
    return product_call(
        mirror_kernel,
        "mirror",
        tiles,
        field,
        indices,
        jax.ShapeDtypeStruct((slots, width), jnp.bfloat16),
        [
            pltpu.VMEM((2 * fibres, NRHS, tiles.shape[1]), jnp.float32),
        ]
        + sum_scratch(slots),
    )


def fill_far(field_ref, far_ref):
    slots, width = field_ref.shape
    unknowns = width // NRHS
    piece = unknowns // SHARES
    step = 32
    field = field_ref[...].astype(jnp.float32)
    blank = jnp.zeros((slots, LANES - unknowns), jnp.float32)
    for r in range(NRHS):
        part = field[:, r * unknowns : (r + 1) * unknowns]
        far_ref[:slots, r, :] = jnp.concatenate([part, blank], axis=1)

    def spread(loop, carry):
        at = loop * step
        whole = far_ref[pl.ds(at, step)].reshape(step * NRHS, LANES)
        there = lane_window(whole.shape, unknowns, LANES)
        for share in range(SHARES):
            part = pltpu.roll(whole, (unknowns - share * piece) % LANES, 1)
            part = jnp.where(there, part, 0.0)
            far_ref[pl.ds((1 + share) * slots + at, step)] = part.reshape(step, NRHS, LANES)
        return carry

    lax.fori_loop(0, slots // step, spread, 0)


def direct_kernel(
    own_at, slot_at, tile_ref, field_ref, own_ref, held_ref, ready, far_ref, *sums
):
    open_stream(tile_ref, held_ref, ready)
    slots, width = field_ref.shape
    unknowns = width // NRHS
    clear(sums)
    fill_far(field_ref, far_ref)
    none = [jnp.zeros((NRHS, LANES), jnp.float32)] * 4

    def product(held, chunk):
        share, host_at, guest_at = tiles_of(chunk)
        pairs = range(0, PAIRS_PER_CHUNK, 2)
        found = []
        for pair in pairs:
            far = []
            for t in range(4):
                far.append(far_ref[slot_at[host_at + 2 * pair + t]])
                far.append(far_ref[slot_at[guest_at + 2 * pair + t] + (1 + share) * slots])
            left = jnp.concatenate(
                [
                    jnp.concatenate(far[:4] + none, axis=0),
                    jnp.concatenate(none + far[4:], axis=0),
                ],
                axis=1,
            ).astype(jnp.bfloat16)
            right = jnp.concatenate([held[pair], held[pair + 1]], axis=1)
            found.append(
                lax.dot_general(
                    left, right, (((1,), (1,)), ((), ())), preferred_element_type=jnp.float32
                )
            )
        for pair, one in zip(pairs, found):
            for t in range(4):
                for m, first in enumerate((host_at, guest_at)):
                    rows = one[(2 * t + m) * NRHS : (2 * t + m + 1) * NRHS]
                    own = own_at[first + 2 * pair + t]
                    if t % 2 == 0:
                        sums[m][own] += rows[:, :LANES]
                    else:
                        sums[2 + m][own] += rows

    run_stream(tile_ref, held_ref, ready, product)
    rows = [
        (sums[0][:, r, :] + sums[1][:, r, :])[:, :unknowns]
        + (sums[2][:, r, :] + sums[3][:, r, :])[:, unknowns:]
        for r in range(NRHS)
    ]
    own_ref[...] = jnp.concatenate(rows, axis=1)


def direct(tiles, field, indices, fibres):
    slots, width = field.shape
    return product_call(
        direct_kernel,
        "direct",
        tiles,
        field,
        indices,
        jax.ShapeDtypeStruct((fibres, width), jnp.float32),
        [
            pltpu.VMEM((HOSTS * slots, NRHS, LANES), jnp.float32),
            pltpu.VMEM((fibres, NRHS, LANES), jnp.float32),
            pltpu.VMEM((fibres, NRHS, LANES), jnp.float32),
            pltpu.VMEM((fibres, NRHS, tiles.shape[1]), jnp.float32),
            pltpu.VMEM((fibres, NRHS, tiles.shape[1]), jnp.float32),
        ],
    )


def per_device(forces, tiles, tile_local, tile_slot, tile_flag, want_list):
    fibres, row_width = forces.shape
    _, peers, capacity = want_list.shape
    slots = peers * capacity

    def exchange(rows):
        return lax.all_to_all(rows, "row", 0, 0, tiled=True)

    direct_at = (tile_local, tile_slot)
    mirror_at = (tile_local, tile_slot, tile_flag)
    chunks = tiles.shape[0] // (HOSTS * LANES) * SHARES
    relay_part = functools.partial(
        relay_mirror, tiles.transpose(1, 2, 0), forces, mirror_at, slots
    )

    asked = exchange(want_list[0])
    *part, echo = relay_part(0, chunks // 2)
    asked, part, echo = lax.optimization_barrier((asked, part, echo))
    asked = asked.reshape(slots)
    asked_pick = (asked[:, None] == jnp.arange(fibres, dtype=jnp.int32)[None, :]).astype(
        jnp.bfloat16
    )
    def fetch(current):
        rows = jnp.dot(asked_pick, current, preferred_element_type=jnp.float32)
        return exchange(rows.astype(jnp.bfloat16))

    def give_back(slot_part):
        return lax.dot_general(
            asked_pick, exchange(slot_part), (((0,), (0,)), ((), ())), preferred_element_type=jnp.float32
        )

    far = fetch(echo)
    wide, slot_part = relay_part(chunks // 2, chunks - chunks // 2, part)
    own_part = direct(wide, far, direct_at, fibres)
    krylov_one = (own_part + give_back(slot_part)).astype(jnp.bfloat16)

    far = fetch(krylov_one)
    slot_part = mirror(wide, krylov_one, mirror_at, slots)
    own_part = direct(wide, far, direct_at, fibres)
    krylov_two = (own_part + give_back(slot_part)).astype(jnp.bfloat16)
    return (krylov_one, krylov_two)


def solution(mesh):
    spec = ("groups", "row")
    in_specs = (
        P(spec, None),
        P(spec, None, None),
        P(spec),
        P(spec),
        P(spec),
        P(spec, None, None),
    )
    out_specs = (P(spec, None), P(spec, None))
    return jax.shard_map(
        per_device, mesh=mesh, in_specs=in_specs, out_specs=out_specs, check_vma=False
    )
```
